512 devices in a mesh: rows: 32 (over y_hi, z, core), cols: 16 (over y_lo, x).
Axes of the slice: x: 4, y: 8 (y_hi: 2, y_lo: 4; y = y_hi * 4 + y_lo), z: 8, core: 2. Of those that a mesh axis runs over, the one named last changes fastest.
Arguments:
- jac: bfloat16 [32768, 1024], P(('rows', 'cols')), may hold values from -0.29882812 to 0.29882812
- panel_jac: bfloat16 [32768, 512], P(('rows', 'cols')), may hold values from -6 to 6
- weights: float32 [32768], P(('rows', 'cols')), may hold values from 0.1 to 1
- tile_lists: int32 [1024, 4], P(('rows', 'cols')), may hold values from 0 to 95, as said below
- tile_masks: int32 [1024, 4], P(('rows', 'cols')), may hold values from 0 to 1
- tile_order: int32 [96], replicated, may hold values from 0 to 95, as said below
- factor_inverse: float32 [512, 512], replicated, as said below
Outputs:
- panel_factor: float32 [96, 256, 512], P('cols', 'rows')
The draws below stay inside these ranges and needn't reach their ends.
Inputs may be any that keep to these rules, and one draw needn't show every extreme that they name: `tile_order`: a permutation of 0 to 95. `tile_lists`: the 4 tiles of one row block are distinct; among the active slots of one device's 2 row blocks, at most 2 name tiles whose positions i share i // 6; in every draw every device has 2 such slots for one and the same position range. `factor_inverse`: lower triangular with a positive diagonal.
All inputs are finite; a program needn't handle non-finite values.
Results may differ from the reference program's by a relative error of at most 0.0029.
Values may be sent and summed in bfloat16 or wider, within the bound.
A program may use at most 64 MiB of HBM per device.

```python
import math
import jax
import jax.numpy as jnp
from jax import lax

TILE = 256
NT = 96
PANEL = 512
KT = 4
RB = 32
NB_DEV = 2
NBLK = 1024
ROWS_ALL = 32768
TPC = 6
SLOTS = 8
CAP = 2
N_COLS = 16


def tile_plan(key):
    base_key = jax.random.fold_in(key, 11)
    tile_perm = jax.random.permutation(jax.random.fold_in(base_key, 1), NT).astype(jnp.int32)
    devices = NBLK // NB_DEV
    bundles = SLOTS // CAP
    owner_ids = jnp.arange(N_COLS, dtype=jnp.int32)
    ranking = jax.random.permutation(jax.random.fold_in(base_key, 2), N_COLS).astype(jnp.int32)
    favored = (ranking == 0).astype(jnp.int32)
    heavy_owner = (ranking < max(1, N_COLS // 4)).astype(jnp.int32)
    scores = jax.random.randint(jax.random.fold_in(base_key, 3), (devices, N_COLS), 0, 1024)
    scores = scores + heavy_owner[None, :] * jax.random.randint(jax.random.fold_in(base_key, 4), (devices, N_COLS), 0, 2048)
    scores = (scores + favored[None, :] * 4096) * N_COLS + owner_ids[None, :]
    unused, groups = lax.top_k(scores, bundles)
    offset_scores = jax.random.randint(jax.random.fold_in(base_key, 5), (devices, bundles, TPC), 0, 65536)
    offset_scores = offset_scores * TPC + jnp.arange(TPC, dtype=jnp.int32)
    unused_too, offsets = lax.top_k(offset_scores, CAP)
    places = (groups[:, :, None].astype(jnp.int32) * TPC + offsets.astype(jnp.int32)).reshape(NBLK, KT)
    return (tile_perm, tile_perm[places].astype(jnp.int32))


def draw_tile_order(key, part):
    return tile_plan(key)[0]


def draw_tile_lists(key, part):
    return tile_plan(key)[1]


def draw_tile_masks(key, part):
    devices = NBLK // NB_DEV
    coins = jax.random.randint(jax.random.fold_in(key, 13), (devices, SLOTS), 0, 8)
    slot_index = jnp.arange(SLOTS, dtype=jnp.int32)[None, :]
    active = jnp.where(slot_index < CAP, 1, jnp.where(coins > 0, 1, 0))
    return active.reshape(NBLK, KT).astype(jnp.int32)


def draw_factor_inverse(key, part):
    row_index = lax.broadcasted_iota(jnp.int32, (PANEL, PANEL), 0)
    col_index = lax.broadcasted_iota(jnp.int32, (PANEL, PANEL), 1)
    diagonal_part = jnp.exp(jax.random.uniform(jax.random.fold_in(key, 21), (PANEL, PANEL), jnp.float32, math.log(0.5), math.log(2.0)))
    spread = jax.random.normal(jax.random.fold_in(key, 22), (PANEL, PANEL), jnp.float32)
    lower_part = spread * (1.0 / math.sqrt(PANEL))
    result = jnp.where(row_index > col_index, lower_part, jnp.where(row_index == col_index, diagonal_part, 0.0))
    return result.astype(jnp.float32)


def block_scale(own_key, extent, shards, smallest, largest):
    loudness, own = 1.0, jax.random.fold_in(own_key, 6)
    for position, shards_of in shards:
        steps = jnp.exp(jax.random.uniform(jax.random.fold_in(own, position), (shards_of,), jnp.float32, smallest / len(shards), largest / len(shards)))
        loudness = loudness * jnp.repeat(steps, extent[position] // shards_of).reshape([-1 if axis == position else 1 for axis in range(len(extent))])
    return loudness


def normal_values(stream_key, dims, width, reach, pieces=(), kind=jnp.bfloat16):
    entries = width * jax.random.normal(stream_key, dims, jnp.float32)
    if pieces:
        entries = entries * block_scale(stream_key, dims, pieces, -0.22, 0.18)
    return jnp.clip(entries, -reach, reach).astype(kind)


def setup_inputs(seed: int = 0) -> dict:
    key_list = jax.random.split(jax.random.key(seed), 8)
    return {
        "jac": normal_values(key_list[0], (ROWS_ALL, KT * TILE), 0.05, 0.29882812, ((0, 512),)),
        "panel_jac": normal_values(key_list[1], (ROWS_ALL, PANEL), 1.0, 6.0, ((0, 512),)),
        "weights": jnp.clip(jnp.exp(math.log(1.0) - 2.3025851 * jax.random.uniform(key_list[2], (ROWS_ALL,), jnp.float32) ** block_scale(key_list[2], (ROWS_ALL,), ((0, 512),), -0.2, 0.2)), 0.1, 1.0),
        "tile_lists": draw_tile_lists(jax.random.fold_in(key_list[7], 71), 0),
        "tile_masks": draw_tile_masks(jax.random.fold_in(key_list[7], 71), 0),
        "tile_order": draw_tile_order(jax.random.fold_in(key_list[7], 71), 0),
        "factor_inverse": draw_factor_inverse(jax.random.fold_in(key_list[7], 71), 0),
    }


def tile_positions(tile_lists, tile_order):
    tile_count = tile_order.shape[0]
    matches = tile_lists[:, :, None] == tile_order[None, None, :]
    return jnp.sum(jnp.where(matches, jnp.arange(tile_count, dtype=jnp.int32), 0), axis=2).astype(jnp.int32)


def reference(jac, panel_jac, weights, tile_lists, tile_masks, tile_order, factor_inverse):
    places = tile_positions(tile_lists, tile_order)
    weighted = (weights[:, None] * panel_jac).astype(jnp.bfloat16)
    group_size = 32
    steps_count = NBLK // group_size
    columns = jac.reshape(steps_count, group_size, RB, KT, TILE)
    panels = weighted.reshape(steps_count, group_size, RB, PANEL)
    place_groups = places.reshape(steps_count, group_size * KT)
    mask_groups = tile_masks.reshape(steps_count, group_size, KT).astype(jnp.float32)

    def add_group(totals, inputs):
        column_group, panel_group, place_group, mask_group = inputs
        terms = jnp.einsum("brkt,brp->bktp", column_group.astype(jnp.float32), panel_group.astype(jnp.float32), precision=lax.Precision.HIGHEST)
        terms = terms * mask_group[:, :, None, None]
        return totals.at[place_group].add(terms.reshape(group_size * KT, TILE, PANEL)), None

    gram_tiles, unused = lax.scan(add_group, jnp.zeros((NT, TILE, PANEL), jnp.float32), (columns, panels, place_groups, mask_groups))
    return jnp.einsum("ntp,qp->ntq", gram_tiles, factor_inverse, precision=lax.Precision.HIGHEST)
```

```python
import functools

import jax
import jax.numpy as jnp
from jax import lax
from jax.experimental import pallas as pl
from jax.experimental.pallas import tpu as pltpu
from jax.sharding import PartitionSpec as P

MESH = pl.DeviceIdType.MESH
F32, BF16 = jnp.float32, jnp.bfloat16
X, YL, YH, Z, H = 4, 4, 2, 8, 2
ZH, Y = Z * H, YH * YL
KT, RB, NB, PER = 4, 32, 2, 6
ROWS, TILE, PANEL = NB * RB, 256, 512
M8 = TILE // (YH * ZH)
M = YH * M8
Q = PANEL // X
BT = X * NB
SL = KT * BT
NT = X * YL * PER
RS = M8 * X * PER


def kernel(
    jac, panel, weights, lists, masks, order, finv_hbm, out,
    ws, wk, jm, jx, px, finv, fhi, flo, bd, phi, plo, gy, ysend, yrecv, red, fs, fx,
    s_wx, r_wx, s_jz, r_jz, s_pz, r_pz, s_jx, r_jx, s_px, r_px,
    s_rp, r_rp, s_rm, r_rm, s_sb, r_sb, s_y, r_y, s_f, r_f, s_fin,
):
    ri, ci = lax.axis_index("rows"), lax.axis_index("cols")
    yh, zh = ri // ZH, ri % ZH
    z, h = zh // H, zh % H
    yl, x = ci // X, ci % X
    y = yh * YL + yl

    def at_x(d):
        return (ri, yl * X + (x + d) % X)

    def at_zh(d):
        return (yh * ZH + (zh + d) % ZH, ci)

    def at_z(d):
        return (yh * ZH + ((z + d) % Z) * H + h, ci)

    def at_y(d):
        other = (y + d) % Y
        return ((other // YL) * ZH + zh, (other % YL) * X + x)

    sibling = (yh * ZH + z * H + (1 - h), ci)

    def send(src, dst, s, r, to):
        copy = pltpu.make_async_remote_copy(src, dst, s, r, device_id=to, device_id_type=MESH)
        copy.start()

    def arrived(ref, sem):
        pltpu.make_async_copy(ref, ref, sem).wait()

    fin_copy = pltpu.make_async_copy(finv_hbm, finv, s_fin)
    fin_copy.start()
    barrier = pltpu.get_barrier_semaphore()

    def greet(n, where):
        def one(d, carry):
            pl.semaphore_signal(barrier, inc=1, device_id=where(d), device_id_type=MESH)
            return carry

        lax.fori_loop(1, n, one, 0)

    greet(X, at_x)
    greet(ZH, at_zh)
    greet(Y, at_y)

    eye = lax.broadcasted_iota(jnp.int32, (ROWS, ROWS), 0) == lax.broadcasted_iota(jnp.int32, (ROWS, ROWS), 1)
    wcol = jnp.sum(jnp.where(eye, jnp.broadcast_to(weights[...], (ROWS, ROWS)), 0.0), axis=1, keepdims=True)
    for q in range(X):
        ws[q] = (wcol * panel[:, q * Q : (q + 1) * Q].astype(F32)).astype(BF16)
    wk[zh, x] = ws[x]

    turned = []
    for k in range(KT):
        both = jnp.concatenate(
            [jac[:, k * TILE + half * 128 : k * TILE + half * 128 + 128].astype(F32) for half in range(YH)], axis=0
        )
        turned.append(both.T.reshape(ZH, M8, YH * ROWS))
    jm[...] = jnp.concatenate(turned, axis=1).astype(BF16)
    jx[x, zh] = jm[zh]

    lane = lax.broadcasted_iota(jnp.int32, (1, 128), 1)
    ids = order[...]
    place = lax.broadcasted_iota(jnp.int32, (1, NT), 1).astype(F32) + 1.0
    base = (zh % 4) * SL + x * NB
    note = jnp.zeros((1, 128), F32)
    for b in range(NB):
        for k in range(KT):
            hit = jnp.sum(jnp.where(ids == lists[b, k], place, 0.0), axis=1, keepdims=True)
            hit = hit * masks[b, k].astype(F32)
            note = note + jnp.where(lane == base + k * BT + b, hit, 0.0)
    px[x, zh] = note

    pl.semaphore_wait(barrier, X - 1 + ZH - 1 + Y - 1)

    for d in range(1, X):
        send(ws.at[(x + d) % X], wk.at[zh, x], s_wx, r_wx, at_x(d))

    def spread(d, carry):
        send(jm.at[(zh + d) % ZH], jx.at[x, zh], s_jz, r_jz, at_zh(d))
        send(px.at[x, zh], px.at[x, zh], s_pz, r_pz, at_zh(d))
        return carry

    lax.fori_loop(1, ZH, spread, 0)

    arrived(wk.at[zh, pl.ds(0, X - 1)], r_wx)
    send(wk.at[zh], wk.at[zh], s_rp.at[0], r_rp.at[0], at_z(1))
    send(wk.at[zh], wk.at[zh], s_rm.at[0], r_rm.at[0], at_z(Z - 1))
    send(wk.at[zh], wk.at[zh], s_sb.at[0], r_sb.at[0], sibling)

    arrived(jx.at[x, pl.ds(0, ZH - 1)], r_jz)
    arrived(px.at[x, pl.ds(0, ZH - 1)], r_pz)
    for d in range(1, X):
        send(jx.at[x], jx.at[x], s_jx, r_jx, at_x(d))
        send(px.at[x], px.at[x], s_px, r_px, at_x(d))

    up, down = Z // 2, Z // 2 - 1
    for s in range(1, up + 1):
        mine = wk.at[((z + Z - s) % Z) * H + h]
        arrived(mine, r_rp.at[s - 1])
        if s < up:
            send(mine, mine, s_rp.at[s], r_rp.at[s], at_z(1))
        send(mine, mine, s_sb.at[s], r_sb.at[s], sibling)
        if s <= down:
            mine = wk.at[((z + s) % Z) * H + h]
            arrived(mine, r_rm.at[s - 1])
            if s < down:
                send(mine, mine, s_rm.at[s], r_rm.at[s], at_z(Z - 1))
            send(mine, mine, s_sb.at[up + s], r_sb.at[up + s], sibling)

    fin_copy.wait()
    full = finv[...]
    high = full.astype(BF16)
    fhi[...] = high
    flo[...] = (full - high.astype(F32)).astype(BF16)

    arrived(jx.at[pl.ds(0, X - 1)], r_jx)
    arrived(px.at[pl.ds(0, X - 1)], r_px)
    for s in range(Z):
        arrived(wk.at[0], r_sb.at[s])

    low_lanes = lax.broadcasted_iota(jnp.int32, (KT * M8, 128), 1) < ROWS
    own_block = (lax.broadcasted_iota(jnp.int32, (BT, X * ROWS), 1) // RB) == lax.broadcasted_iota(
        jnp.int32, (BT, X * ROWS), 0
    )

    def product(t, carry):
        parts = [jx[i, t].astype(F32) for i in range(X)]
        swapped = [pltpu.roll(v, ROWS, 1) for v in parts]
        for half in range(YH):
            if half == 0:
                tiles = [jnp.where(low_lanes, parts[i], swapped[i + 1]) for i in range(0, X, 2)]
            else:
                tiles = [jnp.where(low_lanes, swapped[i], parts[i + 1]) for i in range(0, X, 2)]
            rows = jnp.concatenate(tiles, axis=1)
            for m in range(M8):
                for k in range(KT):
                    row = jnp.broadcast_to(rows[k * M8 + m : k * M8 + m + 1, :], (BT, X * ROWS))
                    at = (half * M8 + m) * SL + k * BT
                    bd[at : at + BT, :] = jnp.where(own_block, row, 0.0)
        terms = jnp.dot(
            bd[...].astype(BF16), wk[t].reshape(X * ROWS, Q), preferred_element_type=F32
        )
        top = terms.astype(BF16)
        rest = (terms - top.astype(F32)).astype(BF16)
        where = pl.ds(pl.multiple_of(t * SL, SL), SL)
        phi[:, where, :] = top.reshape(M, SL, Q)
        plo[:, where, :] = rest.reshape(M, SL, Q)
        return carry

    lax.fori_loop(0, ZH, product, 0)

    notes = []
    for g in range(ZH // 4):
        total = jnp.zeros((1, 128), F32)
        for i in range(X):
            for t in range(4):
                total = total + px[i, g * 4 + t]
        notes.append(total)
    slot_place = jnp.concatenate(notes, axis=1)
    wanted = lax.broadcasted_iota(jnp.int32, (NT, ZH * SL), 0).astype(F32) + 1.0
    chosen = jnp.where(wanted == slot_place, 1.0, 0.0).astype(BF16)

    for half in range(YH):
        for m in range(M8):
            here = half * M8 + m
            gram = jnp.dot(chosen, phi[here], preferred_element_type=F32) + jnp.dot(
                chosen, plo[here], preferred_element_type=F32
            )
            for low in range(YL):
                gy[half * YL + low, m * X * PER : (m + 1) * X * PER, :] = gram[low * X * PER : (low + 1) * X * PER, :]
    for i in range(Y):
        ysend[i] = gy[i].astype(BF16)

    for d in range(1, Y):
        send(ysend.at[(y + d) % Y], yrecv.at[d - 1], s_y, r_y, at_y(d))
    arrived(yrecv, r_y)
    total = gy[y]
    for d in range(Y - 1):
        total = total + yrecv[d].astype(F32)
    red[...] = total
    for i in range(X):
        for j in range(PER):
            fs[i, j] = red[pl.ds(i * PER + j, M8, stride=X * PER), :]
    fx[x] = fs[x]
    for d in range(1, X):
        send(fs.at[(x + d) % X], fx.at[x], s_f, r_f, at_x(d))
    arrived(fx.at[pl.ds(0, X - 1)], r_f)
    gram = jnp.concatenate([fx[i].reshape(PER * M8, Q) for i in range(X)], axis=1)
    ghi = gram.astype(BF16)
    glo = (gram - ghi.astype(F32)).astype(BF16)

    def times(a, b):
        return lax.dot_general(a, b[...], (((1,), (1,)), ((), ())), preferred_element_type=F32)

    out[...] = (times(ghi, fhi) + (times(ghi, flo) + times(glo, fhi))).reshape(PER, M8, PANEL)

    arrived(ws.at[pl.ds(0, X - 1)], s_wx)
    arrived(jm.at[pl.ds(0, ZH - 1)], s_jz)
    arrived(px.at[x, pl.ds(0, ZH - 1)], s_pz)
    arrived(jx.at[pl.ds(0, X - 1)], s_jx)
    arrived(px.at[pl.ds(0, X - 1)], s_px)
    for s in range(up):
        arrived(wk.at[0], s_rp.at[s])
    for s in range(down):
        arrived(wk.at[0], s_rm.at[s])
    for s in range(Z):
        arrived(wk.at[0], s_sb.at[s])
    arrived(yrecv, s_y)
    arrived(fx.at[pl.ds(0, X - 1)], s_f)


def local(jac, panel_jac, weights, tile_lists, tile_masks, tile_order, factor_inverse):
    vmem, smem = pl.BlockSpec(memory_space=pltpu.VMEM), pl.BlockSpec(memory_space=pltpu.SMEM)
    dma = pltpu.SemaphoreType.DMA
    return pl.pallas_call(
        kernel,
        out_shape=jax.ShapeDtypeStruct((PER, M8, PANEL), F32),
        in_specs=[vmem, vmem, vmem, smem, smem, vmem, pl.BlockSpec(memory_space=pl.ANY)],
        out_specs=vmem,
        scratch_shapes=[
            pltpu.VMEM((X, ROWS, Q), BF16),
            pltpu.VMEM((ZH, X, ROWS, Q), BF16),
            pltpu.VMEM((ZH, KT * M8, YH * ROWS), BF16),
            pltpu.VMEM((X, ZH, KT * M8, YH * ROWS), BF16),
            pltpu.VMEM((X, ZH, 1, 128), F32),
            pltpu.VMEM((PANEL, PANEL), F32),
            pltpu.VMEM((PANEL, PANEL), BF16),
            pltpu.VMEM((PANEL, PANEL), BF16),
            pltpu.VMEM((M * SL, X * ROWS), F32),
            pltpu.VMEM((M, ZH * SL, Q), BF16),
            pltpu.VMEM((M, ZH * SL, Q), BF16),
            pltpu.VMEM((Y, RS, Q), F32),
            pltpu.VMEM((Y, RS, Q), BF16),
            pltpu.VMEM((Y - 1, RS, Q), BF16),
            pltpu.VMEM((RS, Q), F32),
            pltpu.VMEM((X, PER, M8, Q), F32),
            pltpu.VMEM((X, PER, M8, Q), F32),
            *[dma(()) for _ in range(10)],
            dma((Z // 2,)), dma((Z // 2,)), dma((Z // 2,)), dma((Z // 2,)), dma((Z,)), dma((Z,)),
            *[dma(()) for _ in range(5)],
        ],
        compiler_params=pltpu.CompilerParams(
            collective_id=0, has_side_effects=True, vmem_limit_bytes=40 * 1024 * 1024
        ),
    )(jac, panel_jac, weights[None, :], tile_lists, tile_masks, tile_order[None, :], factor_inverse)


def solution(mesh):
    in_specs = (
        P(("rows", "cols"), None),
        P(("rows", "cols"), None),
        P(("rows", "cols")),
        P(("rows", "cols"), None),
        P(("rows", "cols"), None),
        P(),
        P(),
    )
    out_specs = P("cols", "rows", None)
    return jax.shard_map(local, mesh=mesh, in_specs=in_specs, out_specs=out_specs, check_vma=False)
```

```python
import functools

import jax
import jax.numpy as jnp
from jax import lax
from jax.experimental import pallas as pl
from jax.experimental.pallas import tpu as pltpu
from jax.sharding import PartitionSpec as P

MESH = pl.DeviceIdType.MESH
F32, BF16 = jnp.float32, jnp.bfloat16
X, YL, YH, Z, H = 4, 4, 2, 8, 2
ZH, Y = Z * H, YH * YL
KT, RB, NB, PER = 4, 32, 2, 6
ROWS, TILE, PANEL = NB * RB, 256, 512
M8 = TILE // (YH * ZH)
M = YH * M8
Q = PANEL // X
BT = X * NB
SL = KT * BT
NT = X * YL * PER


def kernel(
    jac_hbm, panel_hbm, weights_hbm, lists_hbm, masks_hbm, order_hbm, finv_hbm, out,
    jac, panel, weights, lists, masks, order,
    ws, wk, jm, jx, px, finv, fhi, flo, bd, phi, plo, gy, ysend, yrecv,
    s_in, s_wx, r_wx, s_jz, r_jz, s_pz, r_pz, s_jx, r_jx, s_px, r_px,
    s_h, r_near, r_far, r_half, s_sb, r_sb, s_y, r_y,
):
    inputs = [
        pltpu.make_async_copy(src, dst, s_in.at[i])
        for i, (src, dst) in enumerate([
            (panel_hbm, panel), (weights_hbm, weights), (jac_hbm, jac), (lists_hbm, lists),
            (masks_hbm, masks), (order_hbm, order), (finv_hbm, finv),
        ])
    ]
    for copy in inputs:
        copy.start()

    ri, ci = lax.axis_index("rows"), lax.axis_index("cols")
    yh, zh = ri // ZH, ri % ZH
    z, h = zh // H, zh % H
    yl, x = ci // X, ci % X
    y = yh * YL + yl

    def at_x(d):
        return (ri, yl * X + (x + d) % X)

    def at_zh(d):
        return (yh * ZH + (zh + d) % ZH, ci)

    def at_z(d):
        return (yh * ZH + ((z + d) % Z) * H + h, ci)

    def at_yx(there, across):
        return ((there // YL) * ZH + zh, (there % YL) * X + across)

    sibling = (yh * ZH + z * H + (1 - h), ci)

    def send(src, dst, s, r, to):
        copy = pltpu.make_async_remote_copy(src, dst, s, r, device_id=to, device_id_type=MESH)
        copy.start()

    def arrived(ref, sem):
        pltpu.make_async_copy(ref, ref, sem).wait()

    barrier = pltpu.get_barrier_semaphore()

    def greet(n, where):
        def one(d, carry):
            pl.semaphore_signal(barrier, inc=1, device_id=where(d), device_id_type=MESH)
            return carry

        lax.fori_loop(1, n, one, 0)

    greet(ZH, at_zh)
    greet(Y * X, lambda d: at_yx((y + d // X) % Y, (x + d) % X))

    inputs[0].wait()
    inputs[1].wait()
    eye = lax.broadcasted_iota(jnp.int32, (ROWS, ROWS), 0) == lax.broadcasted_iota(jnp.int32, (ROWS, ROWS), 1)
    wcol = jnp.sum(jnp.where(eye, jnp.broadcast_to(weights[...], (ROWS, ROWS)), 0.0), axis=1, keepdims=True)
    for q in range(X):
        ws[q] = (wcol * panel[:, q * Q : (q + 1) * Q].astype(F32)).astype(BF16)

    pl.semaphore_wait(barrier, ZH - 1 + Y * X - 1)

    for d in range(1, X):
        send(ws.at[(x + d) % X], wk.at[zh, x], s_wx, r_wx, at_x(d))
    wk[zh, x] = ws[x]

    inputs[2].wait()
    turned = []
    for k in range(KT):
        both = jnp.concatenate(
            [jac[:, k * TILE + half * 128 : k * TILE + half * 128 + 128].astype(F32) for half in range(YH)], axis=0
        )
        turned.append(both.T.reshape(ZH, M8, YH * ROWS))
    jm[...] = jnp.concatenate(turned, axis=1).astype(BF16)

    def spread(d, carry):
        send(jm.at[(zh + d) % ZH], jx.at[x, zh], s_jz, r_jz.at[z], at_zh(d))
        return carry

    lax.fori_loop(1, ZH, spread, 0)
    jx[x, zh] = jm[zh]

    for copy in inputs[3:6]:
        copy.wait()
    lane = lax.broadcasted_iota(jnp.int32, (1, 128), 1)
    ids = order[...]
    place = lax.broadcasted_iota(jnp.int32, (1, NT), 1).astype(F32) + 1.0
    base = (zh % 4) * SL + x * NB
    note = jnp.zeros((1, 128), F32)
    for b in range(NB):
        for k in range(KT):
            hit = jnp.sum(jnp.where(ids == lists[b, k], place, 0.0), axis=1, keepdims=True)
            hit = hit * masks[b, k].astype(F32)
            note = note + jnp.where(lane == base + k * BT + b, hit, 0.0)
    px[x, zh] = note

    def tell(d, carry):
        send(px.at[x, zh], px.at[x, zh], s_pz, r_pz, at_zh(d))
        return carry

    lax.fori_loop(1, ZH, tell, 0)

    arrived(wk.at[zh, pl.ds(0, X - 1)], r_wx)
    for i, d in enumerate((2, Z - 2, 1, Z - 1)):
        send(wk.at[zh], wk.at[zh], s_h, r_near.at[i], at_z(d))
    send(wk.at[zh], wk.at[zh], s_sb, r_sb.at[z], sibling)

    def pass_jac(i, carry):
        zz = (z + (i % 2) * ((i + 1) // 2) + (1 - i % 2) * (Z - i // 2)) % Z
        mine = jx.at[x, pl.ds(zz * H, H)]

        @pl.when(i == 0)
        def _():
            arrived(jx.at[x, pl.ds(0, 1)], r_jz.at[zz])

        @pl.when(i > 0)
        def _():
            arrived(mine, r_jz.at[zz])

        for d in range(1, X):
            send(mine, mine, s_jx, r_jx.at[zz], at_x(d))
        return carry

    lax.fori_loop(0, Z, pass_jac, 0)

    arrived(px.at[x, pl.ds(0, ZH - 1)], r_pz)
    for d in range(1, X):
        send(px.at[x], px.at[x], s_px, r_px, at_x(d))

    def chunk(d):
        return wk.at[((z + d) % Z) * H + h]

    def share(d):
        send(chunk(d), chunk(d), s_sb, r_sb.at[(z + d) % Z], sibling)

    inputs[6].wait()
    full = finv[...]
    high = full.astype(BF16)
    fhi[...] = high
    flo[...] = (full - high.astype(F32)).astype(BF16)

    for i, (d, first, step) in enumerate(((Z - 2, 0, 1), (2, X // 2, Z - 1))):
        arrived(chunk(d), r_near.at[i])
        send(chunk(d), chunk(d), s_h, r_far.at[i], at_z(step))
        part = wk.at[((z + d) % Z) * H + h, pl.ds(first, X // 2)]
        send(part, part, s_h, r_half.at[i], at_z(2 * step))
        share(d)
    for i, d in enumerate((Z - 1, 1)):
        arrived(chunk(d), r_near.at[2 + i])
        share(d)

    low_lanes = lax.broadcasted_iota(jnp.int32, (KT * M8, 128), 1) < ROWS
    own_block = (lax.broadcasted_iota(jnp.int32, (BT, X * ROWS), 1) // RB) == lax.broadcasted_iota(
        jnp.int32, (BT, X * ROWS), 0
    )

    def distance(i):
        return (z + (i % 2) * ((i + 1) // 2) + (1 - i % 2) * (Z - i // 2)) % Z

    def lay_out(t, carry):
        parts = [jx[i, t].astype(F32) for i in range(X)]
        swapped = [pltpu.roll(v, ROWS, 1) for v in parts]
        for half in range(YH):
            if half == 0:
                tiles = [jnp.where(low_lanes, parts[i], swapped[i + 1]) for i in range(0, X, 2)]
            else:
                tiles = [jnp.where(low_lanes, swapped[i], parts[i + 1]) for i in range(0, X, 2)]
            rows = jnp.concatenate(tiles, axis=1)
            for m in range(M8):
                for k in range(0, KT, 2):
                    pair = [
                        jnp.where(own_block, jnp.broadcast_to(rows[r : r + 1, :], (BT, X * ROWS)), 0.0)
                        for r in (k * M8 + m, (k + 1) * M8 + m)
                    ]
                    at = (half * M8 + m) * SL + k * BT
                    bd[t, at : at + 2 * BT, :] = jnp.concatenate(pair, axis=0).astype(BF16)
        return carry

    def lay_out_pair(i, carry):
        zz = distance(i)
        arrived(jx.at[pl.ds(0, X - 1), pl.ds(zz * H, H)], r_jx.at[zz])
        return lax.fori_loop(zz * H, zz * H + H, lay_out, carry)

    def product(t, first, count):
        terms = jnp.dot(
            bd[t, first * SL : (first + count) * SL, :], wk[t].reshape(X * ROWS, Q), preferred_element_type=F32
        )
        top = terms.astype(BF16)
        rest = (terms - top.astype(F32)).astype(BF16)
        where = pl.ds(pl.multiple_of(t * SL, SL), SL)
        phi[first : first + count, where, :] = top.reshape(count, SL, Q)
        plo[first : first + count, where, :] = rest.reshape(count, SL, Q)

    def near_products(i, carry):
        zz = distance(i)
        arrived(wk.at[0], r_sb.at[zz])
        for core in range(H):
            product(zz * H + core, 0, M)
        return carry

    near = 5
    lax.fori_loop(0, near, lay_out_pair, 0)
    lax.fori_loop(0, near, near_products, 0)
    for i, d in enumerate((Z - 3, 3)):
        arrived(chunk(d), r_far.at[i])
        share(d)
    lax.fori_loop(near, Z - 1, lay_out_pair, 0)
    arrived(wk.at[0, pl.ds(0, X // 2)], r_half.at[0])
    arrived(wk.at[0, pl.ds(0, X // 2)], r_half.at[1])
    share(Z // 2)
    lay_out_pair(Z - 1, 0)

    arrived(px.at[pl.ds(0, X - 1)], r_px)
    notes = []
    for g in range(ZH // 4):
        total = jnp.zeros((1, 128), F32)
        for i in range(X):
            for t in range(4):
                total = total + px[i, g * 4 + t]
        notes.append(total)
    slot_place = jnp.concatenate(notes, axis=1)
    wanted = lax.broadcasted_iota(jnp.int32, (NT, ZH * SL), 0).astype(F32) + 1.0
    chosen = jnp.where(wanted == slot_place, 1.0, 0.0).astype(BF16)

    for half in range(YH):

        def far_products(i, carry):
            zz = distance(i)
            if half == 0:
                arrived(wk.at[0], r_sb.at[zz])
            for core in range(H):
                product(zz * H + core, half * M8, M8)
            return carry

        lax.fori_loop(near, Z, far_products, 0)
        for m in range(M8):
            here = half * M8 + m
            gram = jnp.dot(chosen, phi[here], preferred_element_type=F32) + jnp.dot(
                chosen, plo[here], preferred_element_type=F32
            )
            for low in range(YL):
                gy[low, m * X * PER : (m + 1) * X * PER, :] = gram[low * X * PER : (low + 1) * X * PER, :]
        for low in range(YL):
            for i in range(X):
                piece = [gy[low, pl.ds(i * PER + j, M8, stride=X * PER), :] for j in range(PER)]
                ysend[half * YL + low, i] = jnp.concatenate(piece, axis=0).astype(BF16)

        def deliver(n, carry):
            there, across = half * YL + (yl + n // X) % YL, (x + n) % X
            mine = (there == y) & (across == x)

            @pl.when(jnp.logical_not(mine))
            def _():
                send(ysend.at[there, across], yrecv.at[y * X + x], s_y, r_y, at_yx(there, across))

            @pl.when(mine)
            def _():
                yrecv[y * X + x] = ysend[y, x]

            return carry

        lax.fori_loop(0, YL * X, deliver, 0)

    arrived(yrecv.at[pl.ds(0, Y * X - 1)], r_y)
    quarters = []
    for i in range(X):
        total = yrecv[i].astype(F32)
        for other in range(1, Y):
            total = total + yrecv[other * X + i].astype(F32)
        quarters.append(total)
    gram = jnp.concatenate(quarters, axis=1)
    ghi = gram.astype(BF16)
    glo = (gram - ghi.astype(F32)).astype(BF16)

    def times(a, b):
        return lax.dot_general(a, b[...], (((1,), (1,)), ((), ())), preferred_element_type=F32)

    out[...] = (times(ghi, fhi) + (times(ghi, flo) + times(glo, fhi))).reshape(PER, M8, PANEL)

    arrived(ws.at[pl.ds(0, X - 1)], s_wx)
    arrived(jm.at[pl.ds(0, ZH - 1)], s_jz)
    arrived(px.at[x, pl.ds(0, ZH - 1)], s_pz)
    arrived(jx.at[pl.ds(0, X - 1)], s_jx)
    arrived(px.at[pl.ds(0, X - 1)], s_px)
    arrived(wk.at[pl.ds(0, Z - 1)], s_h)
    arrived(wk.at[pl.ds(0, Z)], s_sb)
    arrived(yrecv.at[pl.ds(0, Y * X - 1)], s_y)


def local(jac, panel_jac, weights, tile_lists, tile_masks, tile_order, factor_inverse):
    dma = pltpu.SemaphoreType.DMA
    return pl.pallas_call(
        kernel,
        out_shape=jax.ShapeDtypeStruct((PER, M8, PANEL), F32),
        in_specs=[pl.BlockSpec(memory_space=pltpu.HBM)] * 7,
        out_specs=pl.BlockSpec(memory_space=pltpu.VMEM),
        scratch_shapes=[
            pltpu.VMEM((ROWS, KT * TILE), BF16),
            pltpu.VMEM((ROWS, PANEL), BF16),
            pltpu.VMEM((1, ROWS), F32),
            pltpu.SMEM((NB, KT), jnp.int32),
            pltpu.SMEM((NB, KT), jnp.int32),
            pltpu.VMEM((1, NT), jnp.int32),
            pltpu.VMEM((X, ROWS, Q), BF16),
            pltpu.VMEM((ZH, X, ROWS, Q), BF16),
            pltpu.VMEM((ZH, KT * M8, YH * ROWS), BF16),
            pltpu.VMEM((X, ZH, KT * M8, YH * ROWS), BF16),
            pltpu.VMEM((X, ZH, 1, 128), F32),
            pltpu.VMEM((PANEL, PANEL), F32),
            pltpu.VMEM((PANEL, PANEL), BF16),
            pltpu.VMEM((PANEL, PANEL), BF16),
            pltpu.VMEM((ZH, M * SL, X * ROWS), BF16),
            pltpu.VMEM((M, ZH * SL, Q), BF16),
            pltpu.VMEM((M, ZH * SL, Q), BF16),
            pltpu.VMEM((YL, M8 * X * PER, Q), F32),
            pltpu.VMEM((Y, X, PER * M8, Q), BF16),
            pltpu.VMEM((Y * X, PER * M8, Q), BF16),
            dma((7,)), dma(()), dma(()), dma(()), dma((Z,)), dma(()), dma(()), dma(()), dma((Z,)), dma(()), dma(()),
            dma(()), dma((4,)), dma((2,)), dma((2,)), dma(()), dma((Z,)), dma(()), dma(()),
        ],
        compiler_params=pltpu.CompilerParams(
            collective_id=0, has_side_effects=True, vmem_limit_bytes=60 * 1024 * 1024
        ),
    )(jac, panel_jac, weights[None, :], tile_lists, tile_masks, tile_order[None, :], factor_inverse)


def solution(mesh):
    in_specs = (
        P(("rows", "cols"), None),
        P(("rows", "cols"), None),
        P(("rows", "cols")),
        P(("rows", "cols"), None),
        P(("rows", "cols"), None),
        P(),
        P(),
    )
    out_specs = P("cols", "rows", None)
    return jax.shard_map(local, mesh=mesh, in_specs=in_specs, out_specs=out_specs, check_vma=False)
```

```python
import functools

import jax
import jax.numpy as jnp
from jax import lax
from jax.experimental import pallas as pl
from jax.experimental.pallas import tpu as pltpu
from jax.sharding import PartitionSpec as P

MESH = pl.DeviceIdType.MESH
F32, BF16 = jnp.float32, jnp.bfloat16
X, YL, YH, Z, H = 4, 4, 2, 8, 2
ZH, Y = Z * H, YH * YL
KT, RB, NB, PER = 4, 32, 2, 6
ROWS, TILE, PANEL = NB * RB, 256, 512
M8 = TILE // (YH * ZH)
M = YH * M8
M4 = M8 // 2
Q = PANEL // X
BT = X * NB
SL = KT * BT
NT = X * YL * PER


def kernel(
    jac_hbm, panel_hbm, weights_hbm, lists_hbm, masks_hbm, order_hbm, finv_hbm, out,
    jac, panel, weights, lists, masks, order,
    ws, wk, jm, jx, px, finv, fhi, flo, bd, phi, plo, gy, ysend, yrecv, done,
    s_in, s_w, s_w0, r_w, s_jz, r_jz, s_pz, r_pz, s_jx, r_jx, s_px, r_px,
    s_h, r_far, r_half, s_sb, r_sb, s_y, r_y, ready,
):
    inputs = [
        pltpu.make_async_copy(src, dst, s_in.at[i])
        for i, (src, dst) in enumerate([
            (panel_hbm, panel), (weights_hbm, weights), (lists_hbm, lists), (masks_hbm, masks),
            (order_hbm, order), (jac_hbm, jac), (finv_hbm, finv),
        ])
    ]
    for copy in inputs:
        copy.start()

    ri, ci = lax.axis_index("rows"), lax.axis_index("cols")
    yh, zh = ri // ZH, ri % ZH
    z, h = zh // H, zh % H
    yl, x = ci // X, ci % X
    y = yh * YL + yl

    def at_xz(dx, dz):
        return (yh * ZH + ((z + dz) % Z) * H + h, yl * X + (x + dx) % X)

    def at_x(d):
        return at_xz(d, 0)

    def at_z(d):
        return at_xz(0, d)

    def at_zh(d):
        return (yh * ZH + (zh + d) % ZH, ci)

    def at_yx(there, across):
        return ((there // YL) * ZH + zh, (there % YL) * X + across)

    sibling = (yh * ZH + z * H + (1 - h), ci)

    def send(src, dst, s, r, to):
        copy = pltpu.make_async_remote_copy(src, dst, s, r, device_id=to, device_id_type=MESH)
        copy.start()

    def arrived(ref, sem):
        pltpu.make_async_copy(ref, ref, sem).wait()

    barrier = pltpu.get_barrier_semaphore()

    def greet(n, where):
        for d in range(1, n):
            pl.semaphore_signal(barrier, inc=1, device_id=where(d), device_id_type=MESH)

    for dz in (2, Z - 2, 0, 1, Z - 1):
        greet(X, lambda d: at_xz(d, dz))
    greet(ZH, at_zh)
    greet(Y, lambda d: at_yx((y + d) % Y, x))

    inputs[0].wait()
    inputs[1].wait()
    eye = lax.broadcasted_iota(jnp.int32, (ROWS, ROWS), 0) == lax.broadcasted_iota(jnp.int32, (ROWS, ROWS), 1)
    wcol = jnp.sum(jnp.where(eye, jnp.broadcast_to(weights[...], (ROWS, ROWS)), 0.0), axis=1, keepdims=True)
    for q in range(X):
        ws[q] = (wcol * panel[:, q * Q : (q + 1) * Q].astype(F32)).astype(BF16)

    for copy in inputs[2:5]:
        copy.wait()
    lane = lax.broadcasted_iota(jnp.int32, (1, 128), 1)
    ids = order[...]
    place = lax.broadcasted_iota(jnp.int32, (1, NT), 1).astype(F32) + 1.0
    base = (zh % 4) * SL + x * NB
    note = jnp.zeros((1, 128), F32)
    for b in range(NB):
        for k in range(KT):
            hit = jnp.sum(jnp.where(ids == lists[b, k], place, 0.0), axis=1, keepdims=True)
            hit = hit * masks[b, k].astype(F32)
            note = note + jnp.where(lane == base + k * BT + b, hit, 0.0)
    px[x, zh] = note

    pl.semaphore_wait(barrier, 5 * (X - 1) + ZH - 1 + Y - 1)

    def near(dz, first, sem):
        def one(dx, carry):
            send(ws.at[(x + dx) % X], wk.at[zh, x], sem, r_w.at[z], at_xz(dx, dz))
            return carry

        lax.fori_loop(first, X, one, 0)

    near(2, 0, s_w)
    near(Z - 2, 0, s_w)
    near(0, 1, s_w0)
    wk[zh, x] = ws[x]

    inputs[5].wait()
    turned = []
    for k in range(KT):
        both = [jac[:, k * TILE + i * 128 : k * TILE + i * 128 + 128].astype(F32) for i in range(YH)]
        turned.append(jnp.concatenate(both, axis=0).T)
    first_four = lax.broadcasted_iota(jnp.int32, (ZH * M8, 128), 0) % M8 < M4
    for half in range(2):
        tiles = []
        for k in range(0, KT, 2):
            if half == 0:
                tile = jnp.where(first_four, turned[k], pltpu.roll(turned[k + 1], M4, 0))
            else:
                tile = jnp.where(first_four, pltpu.roll(turned[k], ZH * M8 - M4, 0), turned[k + 1])
            tiles.append(tile.reshape(ZH, M8, 128))
        jm[half] = jnp.concatenate(tiles, axis=1).astype(BF16)

    def spread(half):
        def one(d, carry):
            send(jm.at[half, (zh + d) % ZH], jx.at[half, x, zh], s_jz.at[half], r_jz.at[half, z], at_zh(d))
            return carry

        lax.fori_loop(1, ZH, one, 0)

    spread(0)

    def tell(d, carry):
        send(px.at[x, zh], px.at[x, zh], s_pz, r_pz, at_zh(d))
        return carry

    lax.fori_loop(1, ZH, tell, 0)
    for d in range(1, Y):
        pl.semaphore_signal(ready, inc=1, device_id=at_yx((y + d) % Y, x), device_id_type=MESH)

    spread(1)
    near(1, 0, s_w)
    near(Z - 1, 0, s_w)
    for half in range(YH):
        jx[half, x, zh] = jm[half, zh]

    inputs[6].wait()
    full = finv[...]
    high = full.astype(BF16)
    fhi[...] = high
    flo[...] = (full - high.astype(F32)).astype(BF16)

    def chunk(d):
        return wk.at[((z + d) % Z) * H + h]

    def share(d):
        send(chunk(d), chunk(d), s_sb, r_sb.at[(z + d) % Z], sibling)


    for i, (d, first, step) in enumerate(((Z - 2, 0, 1), (2, X // 2, Z - 1))):
        arrived(chunk(d), r_w.at[(z + d) % Z])
        send(chunk(d), chunk(d), s_h, r_far.at[i], at_z(step))
        part = wk.at[((z + d) % Z) * H + h, pl.ds(first, X // 2)]
        send(part, part, s_h, r_half.at[i], at_z(2 * step))
        share(d)

    def distance(i):
        return (z + (i % 2) * ((i + 1) // 2) + (1 - i % 2) * (Z - i // 2)) % Z

    def pass_jac(half):
        def one(i, carry):
            zz = distance(i)
            mine = jx.at[half, x, pl.ds(zz * H, H)]

            @pl.when(i == 0)
            def _():
                arrived(jx.at[half, x, pl.ds(0, 1)], r_jz.at[half, zz])

            @pl.when(i > 0)
            def _():
                arrived(mine, r_jz.at[half, zz])

            for d in range(1, X):
                send(mine, mine, s_jx.at[half], r_jx.at[half, zz], at_x(d))
            return carry

        lax.fori_loop(0, Z, one, 0)

    pass_jac(0)
    arrived(px.at[x, pl.ds(0, ZH - 1)], r_pz)
    for d in range(1, X):
        send(px.at[x], px.at[x], s_px, r_px, at_x(d))
    arrived(wk.at[0, pl.ds(0, X - 1)], r_w.at[z])
    share(0)
    for d in (Z - 1, 1):
        arrived(chunk(d), r_w.at[(z + d) % Z])
        share(d)
    pass_jac(1)

    low_lanes = lax.broadcasted_iota(jnp.int32, (2 * M8, 128), 1) < ROWS
    own_block = (lax.broadcasted_iota(jnp.int32, (BT, X * ROWS), 1) // RB) == lax.broadcasted_iota(
        jnp.int32, (BT, X * ROWS), 0
    )

    def lay_out(half, t):
        parts = [jx[half, i, t].astype(F32) for i in range(X)]
        swapped = [pltpu.roll(v, ROWS, 1) for v in parts]
        for up in range(YH):
            if up == 0:
                tiles = [jnp.where(low_lanes, parts[i], swapped[i + 1]) for i in range(0, X, 2)]
            else:
                tiles = [jnp.where(low_lanes, swapped[i], parts[i + 1]) for i in range(0, X, 2)]
            rows = jnp.concatenate(tiles, axis=1)
            for m in range(M4):
                for k in range(0, KT, 2):
                    pair = [
                        jnp.where(own_block, jnp.broadcast_to(rows[r : r + 1, :], (BT, X * ROWS)), 0.0)
                        for r in (k * M4 + m, (k + 1) * M4 + m)
                    ]
                    at = (half * M8 + up * M4 + m) * SL + k * BT
                    bd[t, at : at + 2 * BT, :] = jnp.concatenate(pair, axis=0).astype(BF16)

    def product(half, t):
        terms = jnp.dot(
            bd[t, half * M8 * SL : (half + 1) * M8 * SL, :], wk[t].reshape(X * ROWS, Q), preferred_element_type=F32
        )
        top = terms.astype(BF16)
        rest = (terms - top.astype(F32)).astype(BF16)
        where = pl.ds(pl.multiple_of(t * SL, SL), SL)
        phi[half * M8 : (half + 1) * M8, where, :] = top.reshape(M8, SL, Q)
        plo[half * M8 : (half + 1) * M8, where, :] = rest.reshape(M8, SL, Q)

    def lay_out_pair(half):
        def one(i, carry):
            zz = distance(i)
            arrived(jx.at[half, pl.ds(0, X - 1), pl.ds(zz * H, H)], r_jx.at[half, zz])
            for core in range(H):
                lay_out(half, zz * H + core)
            return carry

        return one

    def products(half):
        def one(i, carry):
            zz = distance(i)
            if half == 0:
                arrived(wk.at[0], r_sb.at[zz])
            for core in range(H):
                product(half, zz * H + core)
            return carry

        return one

    close = 5
    lax.fori_loop(0, close, lay_out_pair(0), 0)
    lax.fori_loop(0, close, products(0), 0)
    for i, d in enumerate((Z - 3, 3)):
        arrived(chunk(d), r_far.at[i])
        share(d)
    arrived(wk.at[0, pl.ds(0, X // 2)], r_half.at[0])
    arrived(wk.at[0, pl.ds(0, X // 2)], r_half.at[1])
    share(Z // 2)
    lax.fori_loop(close, Z, lay_out_pair(0), 0)

    pl.semaphore_wait(ready, Y - 1)

    arrived(px.at[pl.ds(0, X - 1)], r_px)
    notes = []
    for g in range(ZH // 4):
        total = jnp.zeros((1, 128), F32)
        for i in range(X):
            for t in range(4):
                total = total + px[i, g * 4 + t]
        notes.append(total)
    slot_place = jnp.concatenate(notes, axis=1)
    line = lax.broadcasted_iota(jnp.int32, (NT, ZH * SL), 0)
    wanted = ((line % (YL * X)) * PER + line // (YL * X)).astype(F32) + 1.0
    chosen = jnp.where(wanted == slot_place, 1.0, 0.0).astype(BF16)

    for half in range(YH):
        if half == 0:
            lax.fori_loop(close, Z, products(0), 0)
        else:
            lax.fori_loop(0, Z, lay_out_pair(1), 0)
            lax.fori_loop(0, Z, products(1), 0)
        for up in range(YH):
            for m in range(M4):
                here = half * M8 + up * M4 + m
                gram = jnp.dot(chosen, phi[here], preferred_element_type=F32) + jnp.dot(
                    chosen, plo[here], preferred_element_type=F32
                )
                gy[up, m * NT : (m + 1) * NT, :] = gram
            for c in range(YL * X):
                ysend[half, up * YL * X + c] = gy[up, pl.ds(c, M4 * PER, stride=YL * X), :].astype(BF16)

        def deliver(n, carry):
            there, across = (y + n // X) % Y, (x + n) % X
            send(
                ysend.at[half, there * X + across], yrecv.at[half, y * X + x],
                s_y.at[half], r_y.at[half], at_yx(there, across),
            )
            return carry

        lax.fori_loop(1, Y * X, deliver, 0)
        yrecv[half, y * X + x] = ysend[half, y * X + x]

    for half in range(2):
        arrived(yrecv.at[half, pl.ds(0, Y * X - 1)], r_y.at[half])
        for i in range(X):
            total = yrecv[half, i].astype(F32)
            for other in range(1, Y):
                total = total + yrecv[half, other * X + i].astype(F32)
            done[i, half * M4 * PER : (half + 1) * M4 * PER, :] = total
    quarters = []
    for i in range(X):
        quarters.append(jnp.concatenate([done[i, pl.ds(j, M8, stride=PER), :] for j in range(PER)], axis=0))
    gram = jnp.concatenate(quarters, axis=1)
    ghi = gram.astype(BF16)
    glo = (gram - ghi.astype(F32)).astype(BF16)

    def times(a, b):
        return lax.dot_general(a, b[...], (((1,), (1,)), ((), ())), preferred_element_type=F32)

    out[...] = (times(ghi, fhi) + (times(ghi, flo) + times(glo, fhi))).reshape(PER, M8, PANEL)

    arrived(wk.at[pl.ds(0, 4)], s_w)
    arrived(wk.at[0, pl.ds(0, X - 1)], s_w0)
    for half in range(YH):
        arrived(jm.at[half, pl.ds(0, ZH - 1)], s_jz.at[half])
        arrived(jx.at[half, pl.ds(0, X - 1)], s_jx.at[half])
    arrived(px.at[x, pl.ds(0, ZH - 1)], s_pz)
    arrived(px.at[pl.ds(0, X - 1)], s_px)
    arrived(wk.at[pl.ds(0, 3)], s_h)
    arrived(wk.at[pl.ds(0, Z)], s_sb)
    for half in range(2):
        arrived(yrecv.at[half, pl.ds(0, Y * X - 1)], s_y.at[half])


def local(jac, panel_jac, weights, tile_lists, tile_masks, tile_order, factor_inverse):
    dma = pltpu.SemaphoreType.DMA
    given = (jac, panel_jac, weights[None, :], tile_lists, tile_masks, tile_order[None, :], factor_inverse)
    held = [pltpu.with_memory_space_constraint(value, pltpu.HBM) for value in given]
    return pl.pallas_call(
        kernel,
        out_shape=jax.ShapeDtypeStruct((PER, M8, PANEL), F32),
        in_specs=[pl.BlockSpec(memory_space=pltpu.HBM)] * 7,
        out_specs=pl.BlockSpec(memory_space=pltpu.VMEM),
        scratch_shapes=[
            pltpu.VMEM((ROWS, KT * TILE), BF16),
            pltpu.VMEM((ROWS, PANEL), BF16),
            pltpu.VMEM((1, ROWS), F32),
            pltpu.SMEM((NB, KT), jnp.int32),
            pltpu.SMEM((NB, KT), jnp.int32),
            pltpu.VMEM((1, NT), jnp.int32),
            pltpu.VMEM((X, ROWS, Q), BF16),
            pltpu.VMEM((ZH, X, ROWS, Q), BF16),
            pltpu.VMEM((YH, ZH, 2 * M8, 2 * ROWS), BF16),
            pltpu.VMEM((YH, X, ZH, 2 * M8, 2 * ROWS), BF16),
            pltpu.VMEM((X, ZH, 1, 128), F32),
            pltpu.VMEM((PANEL, PANEL), F32),
            pltpu.VMEM((PANEL, PANEL), BF16),
            pltpu.VMEM((PANEL, PANEL), BF16),
            pltpu.VMEM((ZH, M * SL, X * ROWS), BF16),
            pltpu.VMEM((M, ZH * SL, Q), BF16),
            pltpu.VMEM((M, ZH * SL, Q), BF16),
            pltpu.VMEM((YH, M4 * NT, Q), F32),
            pltpu.VMEM((2, Y * X, M4 * PER, Q), BF16),
            pltpu.VMEM((2, Y * X, M4 * PER, Q), BF16),
            pltpu.VMEM((X, M8 * PER, Q), F32),
            dma((7,)), dma(()), dma(()), dma((Z,)), dma((YH,)), dma((YH, Z)), dma(()), dma(()),
            dma((YH,)), dma((YH, Z)), dma(()), dma(()),
            dma(()), dma((2,)), dma((2,)), dma(()), dma((Z,)), dma((2,)), dma((2,)), pltpu.SemaphoreType.REGULAR,
        ],
        compiler_params=pltpu.CompilerParams(
            collective_id=0, has_side_effects=True, vmem_limit_bytes=48 * 1024 * 1024
        ),
    )(*held)


def solution(mesh):
    in_specs = (
        P(("rows", "cols"), None),
        P(("rows", "cols"), None),
        P(("rows", "cols")),
        P(("rows", "cols"), None),
        P(("rows", "cols"), None),
        P(),
        P(),
    )
    out_specs = P("cols", "rows", None)
    return jax.shard_map(local, mesh=mesh, in_specs=in_specs, out_specs=out_specs, check_vma=False)
```

```python
import functools

import jax
import jax.numpy as jnp
from jax import lax
from jax.experimental import pallas as pl
from jax.experimental.pallas import tpu as pltpu
from jax.sharding import PartitionSpec as P

MESH = pl.DeviceIdType.MESH
F32, BF16 = jnp.float32, jnp.bfloat16
X, YL, YH, Z, H = 4, 4, 2, 8, 2
ZH, Y = Z * H, YH * YL
KT, RB, NB, PER = 4, 32, 2, 6
ROWS, TILE, PANEL = NB * RB, 256, 512
M8 = TILE // (YH * ZH)
M = YH * M8
M4 = M8 // 2
Q = PANEL // X
BT = X * NB
SL = KT * BT
NT = X * YL * PER


def kernel(
    jac_hbm, panel_hbm, weights_hbm, lists_hbm, masks_hbm, order_hbm, finv_hbm, out,
    jac, panel, weights, lists, masks, order,
    ws, wk, jm, jx, px, finv, fhi, flo, bd, terms_of, gy, ysend, yrecv, done,
    s_in, s_w, s_w0, r_w, s_jz, r_jz, s_pz, r_pz, s_jx, r_jx, s_px, r_px,
    s_h, r_far, r_half, s_sb, r_sb, s_y, r_y, ready,
):
    inputs = [
        pltpu.make_async_copy(src, dst, s_in.at[i])
        for i, (src, dst) in enumerate([
            (panel_hbm, panel), (weights_hbm, weights), (lists_hbm, lists), (masks_hbm, masks),
            (order_hbm, order), (jac_hbm, jac), (finv_hbm, finv),
        ])
    ]
    for copy in inputs:
        copy.start()

    ri, ci = lax.axis_index("rows"), lax.axis_index("cols")
    yh, zh = ri // ZH, ri % ZH
    z, h = zh // H, zh % H
    yl, x = ci // X, ci % X
    y = yh * YL + yl

    def at_xz(dx, dz):
        return (yh * ZH + ((z + dz) % Z) * H + h, yl * X + (x + dx) % X)

    def at_x(d):
        return at_xz(d, 0)

    def at_z(d):
        return at_xz(0, d)

    def at_zh(d):
        return (yh * ZH + (zh + d) % ZH, ci)

    def at_yx(there, across):
        return ((there // YL) * ZH + zh, (there % YL) * X + across)

    sibling = (yh * ZH + z * H + (1 - h), ci)

    def send(src, dst, s, r, to):
        copy = pltpu.make_async_remote_copy(src, dst, s, r, device_id=to, device_id_type=MESH)
        copy.start()

    def arrived(ref, sem):
        pltpu.make_async_copy(ref, ref, sem).wait()

    barrier = pltpu.get_barrier_semaphore()

    def greet(n, where):
        for d in range(1, n):
            pl.semaphore_signal(barrier, inc=1, device_id=where(d), device_id_type=MESH)

    for dz in (2, Z - 2, 0, 1, Z - 1):
        greet(X, lambda d: at_xz(d, dz))
    greet(ZH, at_zh)
    greet(Y, lambda d: at_yx((y + d) % Y, x))

    inputs[0].wait()
    inputs[1].wait()
    eye = lax.broadcasted_iota(jnp.int32, (ROWS, ROWS), 0) == lax.broadcasted_iota(jnp.int32, (ROWS, ROWS), 1)
    wcol = jnp.sum(jnp.where(eye, jnp.broadcast_to(weights[...], (ROWS, ROWS)), 0.0), axis=1, keepdims=True)
    for q in range(X):
        ws[q] = (wcol * panel[:, q * Q : (q + 1) * Q].astype(F32)).astype(BF16)

    pl.semaphore_wait(barrier, 5 * (X - 1) + ZH - 1 + Y - 1)

    def near(dz, first, sem):
        def one(dx, carry):
            send(ws.at[(x + dx) % X], wk.at[zh, x], sem, r_w.at[z], at_xz(dx, dz))
            return carry

        lax.fori_loop(first, X, one, 0)

    near(2, 0, s_w)
    near(Z - 2, 0, s_w)
    near(0, 1, s_w0)
    wk[zh, x] = ws[x]

    inputs[5].wait()
    turned = []
    for k in range(KT):
        both = [jac[:, k * TILE + i * 128 : k * TILE + i * 128 + 128].astype(F32) for i in range(YH)]
        turned.append(jnp.concatenate(both, axis=0).T)
    first_four = lax.broadcasted_iota(jnp.int32, (ZH * M8, 128), 0) % M8 < M4
    for half in range(2):
        tiles = []
        for k in range(0, KT, 2):
            if half == 0:
                tile = jnp.where(first_four, turned[k], pltpu.roll(turned[k + 1], M4, 0))
            else:
                tile = jnp.where(first_four, pltpu.roll(turned[k], ZH * M8 - M4, 0), turned[k + 1])
            tiles.append(tile.reshape(ZH, M8, 128))
        jm[half] = jnp.concatenate(tiles, axis=1).astype(BF16)

    def spread(half):
        def one(d, carry):
            send(jm.at[half, (zh + d) % ZH], jx.at[half, x, zh], s_jz.at[half], r_jz.at[half, z], at_zh(d))
            return carry

        lax.fori_loop(1, ZH, one, 0)

    spread(0)

    for copy in inputs[2:5]:
        copy.wait()
    lane = lax.broadcasted_iota(jnp.int32, (1, 128), 1)
    ids = order[...]
    place = lax.broadcasted_iota(jnp.int32, (1, NT), 1).astype(F32) + 1.0
    base = (zh % 4) * SL + x * NB
    note = jnp.zeros((1, 128), F32)
    for b in range(NB):
        for k in range(KT):
            hit = jnp.sum(jnp.where(ids == lists[b, k], place, 0.0), axis=1, keepdims=True)
            hit = hit * masks[b, k].astype(F32)
            note = note + jnp.where(lane == base + k * BT + b, hit, 0.0)
    px[x, zh] = note

    def tell(d, carry):
        send(px.at[x, zh], px.at[x, zh], s_pz, r_pz, at_zh(d))
        return carry

    lax.fori_loop(1, ZH, tell, 0)
    for d in range(1, Y):
        pl.semaphore_signal(ready, inc=1, device_id=at_yx((y + d) % Y, x), device_id_type=MESH)

    spread(1)
    near(1, 0, s_w)
    near(Z - 1, 0, s_w)
    for half in range(YH):
        jx[half, x, zh] = jm[half, zh]

    inputs[6].wait()
    full = finv[...].T
    high = full.astype(BF16)
    fhi[...] = high
    flo[...] = (full - high.astype(F32)).astype(BF16)

    def chunk(d):
        return wk.at[((z + d) % Z) * H + h]

    def share(d):
        send(chunk(d), chunk(d), s_sb, r_sb.at[(z + d) % Z], sibling)


    for i, (d, first, step) in enumerate(((Z - 2, 0, 1), (2, X // 2, Z - 1))):
        arrived(chunk(d), r_w.at[(z + d) % Z])
        send(chunk(d), chunk(d), s_h, r_far.at[i], at_z(step))
        part = wk.at[((z + d) % Z) * H + h, pl.ds(first, X // 2)]
        send(part, part, s_h, r_half.at[i], at_z(2 * step))
        share(d)

    def distance(i):
        return (z + (i % 2) * ((i + 1) // 2) + (1 - i % 2) * (Z - i // 2)) % Z

    def pass_jac(half):
        def one(i, carry):
            zz = distance(i)
            mine = jx.at[half, x, pl.ds(zz * H, H)]

            @pl.when(i == 0)
            def _():
                arrived(jx.at[half, x, pl.ds(0, 1)], r_jz.at[half, zz])

            @pl.when(i > 0)
            def _():
                arrived(mine, r_jz.at[half, zz])

            for d in range(1, X):
                send(mine, mine, s_jx.at[half], r_jx.at[half, zz], at_x(d))
            return carry

        lax.fori_loop(0, Z, one, 0)

    pass_jac(0)
    arrived(px.at[x, pl.ds(0, ZH - 1)], r_pz)
    for d in range(1, X):
        send(px.at[x], px.at[x], s_px, r_px, at_x(d))
    arrived(wk.at[0, pl.ds(0, X - 1)], r_w.at[z])
    share(0)
    for d in (Z - 1, 1):
        arrived(chunk(d), r_w.at[(z + d) % Z])
        share(d)
    pass_jac(1)

    low_lanes = lax.broadcasted_iota(jnp.int32, (2 * M8, 128), 1) < ROWS
    own_block = (lax.broadcasted_iota(jnp.int32, (BT, X * ROWS), 1) // RB) == lax.broadcasted_iota(
        jnp.int32, (BT, X * ROWS), 0
    )

    def lay_out(half, t):
        parts = [jx[half, i, t].astype(F32) for i in range(X)]
        swapped = [pltpu.roll(v, ROWS, 1) for v in parts]
        for up in range(YH):
            if up == 0:
                tiles = [jnp.where(low_lanes, parts[i], swapped[i + 1]) for i in range(0, X, 2)]
            else:
                tiles = [jnp.where(low_lanes, swapped[i], parts[i + 1]) for i in range(0, X, 2)]
            rows = jnp.concatenate(tiles, axis=1)
            for m in range(M4):
                for k in range(0, KT, 2):
                    pair = [
                        jnp.where(own_block, jnp.broadcast_to(rows[r : r + 1, :], (BT, X * ROWS)), 0.0)
                        for r in (k * M4 + m, (k + 1) * M4 + m)
                    ]
                    at = (half * M8 + up * M4 + m) * SL + k * BT
                    bd[t, at : at + 2 * BT, :] = jnp.concatenate(pair, axis=0).astype(BF16)

    def product(half, t):
        terms = jnp.dot(
            bd[t, half * M8 * SL : (half + 1) * M8 * SL, :], wk[t].reshape(X * ROWS, Q), preferred_element_type=F32
        )
        top = terms.astype(BF16)
        rest = (terms - top.astype(F32)).astype(BF16)
        where = pl.ds(pl.multiple_of(t * SL, SL), SL)
        both = jnp.concatenate([top, rest], axis=1)
        terms_of[half * M8 : (half + 1) * M8, where, :] = both.reshape(M8, SL, 2 * Q)

    def lay_out_pair(half):
        def one(i, carry):
            zz = distance(i)
            arrived(jx.at[half, pl.ds(0, X - 1), pl.ds(zz * H, H)], r_jx.at[half, zz])
            for core in range(H):
                lay_out(half, zz * H + core)
            return carry

        return one

    def products(half):
        def one(i, carry):
            zz = distance(i)
            if half == 0:
                arrived(wk.at[0], r_sb.at[zz])
            for core in range(H):
                product(half, zz * H + core)
            return carry

        return one

    close = 5
    lax.fori_loop(0, close, lay_out_pair(0), 0)
    lax.fori_loop(0, close, products(0), 0)
    for i, d in enumerate((Z - 3, 3)):
        arrived(chunk(d), r_far.at[i])
        share(d)
    arrived(wk.at[0, pl.ds(0, X // 2)], r_half.at[0])
    arrived(wk.at[0, pl.ds(0, X // 2)], r_half.at[1])
    share(Z // 2)
    lax.fori_loop(close, Z, lay_out_pair(0), 0)

    pl.semaphore_wait(ready, Y - 1)

    arrived(px.at[pl.ds(0, X - 1)], r_px)
    notes = []
    for g in range(ZH // 4):
        total = jnp.zeros((1, 128), F32)
        for i in range(X):
            for t in range(4):
                total = total + px[i, g * 4 + t]
        notes.append(total)
    slot_place = jnp.concatenate(notes, axis=1)
    line = lax.broadcasted_iota(jnp.int32, (NT, ZH * SL), 0)
    wanted = ((line % (YL * X)) * PER + line // (YL * X)).astype(F32) + 1.0
    chosen = jnp.where(wanted == slot_place, 1.0, 0.0).astype(BF16)

    for half in range(YH):
        if half == 0:
            for i in range(close, Z):
                product(0, distance(i) * H + h)
            for i in range(close, Z):
                arrived(wk.at[0], r_sb.at[distance(i)])
                product(0, distance(i) * H + (1 - h))
        else:
            lax.fori_loop(0, Z, lay_out_pair(1), 0)
            lax.fori_loop(0, Z, products(1), 0)
        for up in range(YH):
            for m in range(M4):
                here = half * M8 + up * M4 + m
                gram = jnp.dot(chosen, terms_of[here], preferred_element_type=F32)
                gy[up, m * NT : (m + 1) * NT, :] = gram[:, :Q] + gram[:, Q:]
            for c in range(YL * X):
                ysend[half, up * YL * X + c] = gy[up, pl.ds(c, M4 * PER, stride=YL * X), :].astype(BF16)

        def deliver(n, carry):
            there, across = (y + n // X) % Y, (x + n) % X
            send(
                ysend.at[half, there * X + across], yrecv.at[half, y * X + x],
                s_y.at[half], r_y.at[half], at_yx(there, across),
            )
            return carry

        lax.fori_loop(1, Y * X, deliver, 0)
        yrecv[half, y * X + x] = ysend[half, y * X + x]

    for half in range(2):
        arrived(yrecv.at[half, pl.ds(0, Y * X - 1)], r_y.at[half])
        for i in range(X):
            total = yrecv[half, i].astype(F32)
            for other in range(1, Y):
                total = total + yrecv[half, other * X + i].astype(F32)
            done[i, half * M4 * PER : (half + 1) * M4 * PER, :] = total
    quarters = []
    for i in range(X):
        quarters.append(jnp.concatenate([done[i, pl.ds(j, M8, stride=PER), :] for j in range(PER)], axis=0))
    gram = jnp.concatenate(quarters, axis=1)
    ghi = gram.astype(BF16)
    glo = (gram - ghi.astype(F32)).astype(BF16)

    wide = jnp.dot(jnp.concatenate([ghi, glo], axis=0), fhi[...], preferred_element_type=F32)
    low = jnp.dot(ghi, flo[...], preferred_element_type=F32)
    out[...] = (wide[: PER * M8] + (wide[PER * M8 :] + low)).reshape(PER, M8, PANEL)

    arrived(wk.at[pl.ds(0, 4)], s_w)
    arrived(wk.at[0, pl.ds(0, X - 1)], s_w0)
    for half in range(YH):
        arrived(jm.at[half, pl.ds(0, ZH - 1)], s_jz.at[half])
        arrived(jx.at[half, pl.ds(0, X - 1)], s_jx.at[half])
    arrived(px.at[x, pl.ds(0, ZH - 1)], s_pz)
    arrived(px.at[pl.ds(0, X - 1)], s_px)
    arrived(wk.at[pl.ds(0, 3)], s_h)
    arrived(wk.at[pl.ds(0, Z)], s_sb)
    for half in range(2):
        arrived(yrecv.at[half, pl.ds(0, Y * X - 1)], s_y.at[half])


def local(jac, panel_jac, weights, tile_lists, tile_masks, tile_order, factor_inverse):
    dma = pltpu.SemaphoreType.DMA
    given = (jac, panel_jac, weights[None, :], tile_lists, tile_masks, tile_order[None, :], factor_inverse)
    held = [pltpu.with_memory_space_constraint(value, pltpu.HBM) for value in given]
    return pl.pallas_call(
        kernel,
        out_shape=jax.ShapeDtypeStruct((PER, M8, PANEL), F32),
        in_specs=[pl.BlockSpec(memory_space=pltpu.HBM)] * 7,
        out_specs=pl.BlockSpec(memory_space=pltpu.VMEM),
        scratch_shapes=[
            pltpu.VMEM((ROWS, KT * TILE), BF16),
            pltpu.VMEM((ROWS, PANEL), BF16),
            pltpu.VMEM((1, ROWS), F32),
            pltpu.SMEM((NB, KT), jnp.int32),
            pltpu.SMEM((NB, KT), jnp.int32),
            pltpu.VMEM((1, NT), jnp.int32),
            pltpu.VMEM((X, ROWS, Q), BF16),
            pltpu.VMEM((ZH, X, ROWS, Q), BF16),
            pltpu.VMEM((YH, ZH, 2 * M8, 2 * ROWS), BF16),
            pltpu.VMEM((YH, X, ZH, 2 * M8, 2 * ROWS), BF16),
            pltpu.VMEM((X, ZH, 1, 128), F32),
            pltpu.VMEM((PANEL, PANEL), F32),
            pltpu.VMEM((PANEL, PANEL), BF16),
            pltpu.VMEM((PANEL, PANEL), BF16),
            pltpu.VMEM((ZH, M * SL, X * ROWS), BF16),
            pltpu.VMEM((M, ZH * SL, 2 * Q), BF16),
            pltpu.VMEM((YH, M4 * NT, Q), F32),
            pltpu.VMEM((2, Y * X, M4 * PER, Q), BF16),
            pltpu.VMEM((2, Y * X, M4 * PER, Q), BF16),
            pltpu.VMEM((X, M8 * PER, Q), F32),
            dma((7,)), dma(()), dma(()), dma((Z,)), dma((YH,)), dma((YH, Z)), dma(()), dma(()),
            dma((YH,)), dma((YH, Z)), dma(()), dma(()),
            dma(()), dma((2,)), dma((2,)), dma(()), dma((Z,)), dma((2,)), dma((2,)), pltpu.SemaphoreType.REGULAR,
        ],
        compiler_params=pltpu.CompilerParams(
            collective_id=0, has_side_effects=True, vmem_limit_bytes=48 * 1024 * 1024
        ),
    )(*held)


def solution(mesh):
    in_specs = (
        P(("rows", "cols"), None),
        P(("rows", "cols"), None),
        P(("rows", "cols")),
        P(("rows", "cols"), None),
        P(("rows", "cols"), None),
        P(),
        P(),
    )
    out_specs = P("cols", "rows", None)
    return jax.shard_map(local, mesh=mesh, in_specs=in_specs, out_specs=out_specs, check_vma=False)
```

```python
import functools

import jax
import jax.numpy as jnp
from jax import lax
from jax.experimental import pallas as pl
from jax.experimental.pallas import tpu as pltpu
from jax.sharding import PartitionSpec as P

MESH = pl.DeviceIdType.MESH
F32, BF16 = jnp.float32, jnp.bfloat16
X, YL, YH, Z, H = 4, 4, 2, 8, 2
ZH, Y = Z * H, YH * YL
KT, RB, NB, PER = 4, 32, 2, 6
ROWS, TILE, PANEL = NB * RB, 256, 512
M8 = TILE // (YH * ZH)
M = YH * M8
M4 = M8 // 2
Q = PANEL // X
BT = X * NB
SL = KT * BT
NT = X * YL * PER


def kernel(
    jac_hbm, panel_hbm, weights_hbm, lists_hbm, masks_hbm, order_hbm, finv_hbm, out,
    jac, panel, weights, lists, masks, order,
    ws, wk, jm, jx, px, finv, fhi, flo, bd, terms_of, gy, ysend, yrecv, done,
    s_in, s_w, s_w0, r_w, s_jz, r_jz, s_pz, r_pz, s_jx, r_jx, s_px, r_px,
    s_h, r_far, r_half, s_sb, r_sb, s_y, r_y, ready,
):
    inputs = [
        pltpu.make_async_copy(src, dst, s_in.at[i])
        for i, (src, dst) in enumerate([
            (panel_hbm, panel), (weights_hbm, weights), (lists_hbm, lists), (masks_hbm, masks),
            (order_hbm, order), (jac_hbm, jac), (finv_hbm, finv),
        ])
    ]
    for copy in inputs:
        copy.start()

    ri, ci = lax.axis_index("rows"), lax.axis_index("cols")
    yh, zh = ri // ZH, ri % ZH
    z, h = zh // H, zh % H
    yl, x = ci // X, ci % X
    y = yh * YL + yl

    def at_xz(dx, dz):
        return (yh * ZH + ((z + dz) % Z) * H + h, yl * X + (x + dx) % X)

    def at_x(d):
        return at_xz(d, 0)

    def at_z(d):
        return at_xz(0, d)

    def at_zh(d):
        return (yh * ZH + (zh + d) % ZH, ci)

    def at_yx(there, across):
        return ((there // YL) * ZH + zh, (there % YL) * X + across)

    sibling = (yh * ZH + z * H + (1 - h), ci)

    def send(src, dst, s, r, to):
        copy = pltpu.make_async_remote_copy(src, dst, s, r, device_id=to, device_id_type=MESH)
        copy.start()

    def arrived(ref, sem):
        pltpu.make_async_copy(ref, ref, sem).wait()

    barrier = pltpu.get_barrier_semaphore()

    def greet(n, where):
        for d in range(1, n):
            pl.semaphore_signal(barrier, inc=1, device_id=where(d), device_id_type=MESH)

    for dz in (2, Z - 2, 0, 1, Z - 1):
        greet(X, lambda d: at_xz(d, dz))
    greet(ZH, at_zh)
    greet(Y, lambda d: at_yx((y + d) % Y, x))

    inputs[0].wait()
    inputs[1].wait()
    eye = lax.broadcasted_iota(jnp.int32, (ROWS, ROWS), 0) == lax.broadcasted_iota(jnp.int32, (ROWS, ROWS), 1)
    wcol = jnp.sum(jnp.where(eye, jnp.broadcast_to(weights[...], (ROWS, ROWS)), 0.0), axis=1, keepdims=True)
    for q in range(X):
        ws[q] = (wcol * panel[:, q * Q : (q + 1) * Q].astype(F32)).astype(BF16)

    pl.semaphore_wait(barrier, 5 * (X - 1) + ZH - 1 + Y - 1)

    def near(dz, first, sem):
        def one(dx, carry):
            send(ws.at[(x + dx) % X], wk.at[zh, x], sem, r_w.at[z], at_xz(dx, dz))
            return carry

        lax.fori_loop(first, X, one, 0)

    near(2, 0, s_w)
    near(Z - 2, 0, s_w)
    near(0, 1, s_w0)
    wk[zh, x] = ws[x]

    inputs[5].wait()
    turned = []
    for k in range(KT):
        both = [jac[:, k * TILE + i * 128 : k * TILE + i * 128 + 128].astype(F32) for i in range(YH)]
        turned.append(jnp.concatenate(both, axis=0).T)
    first_four = lax.broadcasted_iota(jnp.int32, (ZH * M8, 128), 0) % M8 < M4
    for half in range(2):
        tiles = []
        for k in range(0, KT, 2):
            if half == 0:
                tile = jnp.where(first_four, turned[k], pltpu.roll(turned[k + 1], M4, 0))
            else:
                tile = jnp.where(first_four, pltpu.roll(turned[k], ZH * M8 - M4, 0), turned[k + 1])
            tiles.append(tile.reshape(ZH, M8, 128))
        jm[half] = jnp.concatenate(tiles, axis=1).astype(BF16)

    def spread(half):
        def one(d, carry):
            send(jm.at[half, (zh + d) % ZH], jx.at[half, x, zh], s_jz.at[half], r_jz.at[half, z], at_zh(d))
            return carry

        lax.fori_loop(1, ZH, one, 0)

    spread(0)

    for copy in inputs[2:5]:
        copy.wait()
    lane = lax.broadcasted_iota(jnp.int32, (1, 128), 1)
    ids = order[...]
    place = lax.broadcasted_iota(jnp.int32, (1, NT), 1).astype(F32) + 1.0
    base = (zh % 4) * SL + x * NB
    note = jnp.zeros((1, 128), F32)
    for b in range(NB):
        for k in range(KT):
            hit = jnp.sum(jnp.where(ids == lists[b, k], place, 0.0), axis=1, keepdims=True)
            hit = hit * masks[b, k].astype(F32)
            note = note + jnp.where(lane == base + k * BT + b, hit, 0.0)
    px[x, zh] = note

    def tell(d, carry):
        send(px.at[x, zh], px.at[x, zh], s_pz, r_pz, at_zh(d))
        return carry

    lax.fori_loop(1, ZH, tell, 0)
    for d in range(1, Y):
        pl.semaphore_signal(ready, inc=1, device_id=at_yx((y + d) % Y, x), device_id_type=MESH)

    spread(1)
    near(1, 0, s_w)
    near(Z - 1, 0, s_w)
    for half in range(YH):
        jx[half, x, zh] = jm[half, zh]

    inputs[6].wait()
    full = finv[...].T
    high = full.astype(BF16)
    fhi[...] = high
    flo[...] = (full - high.astype(F32)).astype(BF16)

    def chunk(d):
        return wk.at[((z + d) % Z) * H + h]

    def share(d):
        send(chunk(d), chunk(d), s_sb, r_sb.at[(z + d) % Z], sibling)


    for i, (d, first, step) in enumerate(((Z - 2, 0, 1), (2, X // 2, Z - 1))):
        arrived(chunk(d), r_w.at[(z + d) % Z])
        send(chunk(d), chunk(d), s_h, r_far.at[i], at_z(step))
        part = wk.at[((z + d) % Z) * H + h, pl.ds(first, X // 2)]
        send(part, part, s_h, r_half.at[i], at_z(2 * step))
        share(d)

    def distance(i):
        return (z + (i % 2) * ((i + 1) // 2) + (1 - i % 2) * (Z - i // 2)) % Z

    def pass_jac(half):
        def one(i, carry):
            zz = distance(i)
            mine = jx.at[half, x, pl.ds(zz * H, H)]

            @pl.when(i == 0)
            def _():
                arrived(jx.at[half, x, pl.ds(0, 1)], r_jz.at[half, zz])

            @pl.when(i > 0)
            def _():
                arrived(mine, r_jz.at[half, zz])

            for d in range(1, X):
                send(mine, mine, s_jx.at[half], r_jx.at[half, zz], at_x(d))
            return carry

        lax.fori_loop(0, Z, one, 0)

    pass_jac(0)
    arrived(px.at[x, pl.ds(0, ZH - 1)], r_pz)
    for d in range(1, X):
        send(px.at[x], px.at[x], s_px, r_px, at_x(d))
    arrived(wk.at[0, pl.ds(0, X - 1)], r_w.at[z])
    share(0)
    for d in (Z - 1, 1):
        arrived(chunk(d), r_w.at[(z + d) % Z])
        share(d)
    pass_jac(1)

    low_lanes = lax.broadcasted_iota(jnp.int32, (2 * M8, 128), 1) < ROWS
    own_block = (lax.broadcasted_iota(jnp.int32, (BT, X * ROWS), 1) // RB) == lax.broadcasted_iota(
        jnp.int32, (BT, X * ROWS), 0
    )

    def lay_out(half, t):
        parts = [jx[half, i, t].astype(F32) for i in range(X)]
        swapped = [pltpu.roll(v, ROWS, 1) for v in parts]
        for up in range(YH):
            if up == 0:
                tiles = [jnp.where(low_lanes, parts[i], swapped[i + 1]) for i in range(0, X, 2)]
            else:
                tiles = [jnp.where(low_lanes, swapped[i], parts[i + 1]) for i in range(0, X, 2)]
            rows = jnp.concatenate(tiles, axis=1)
            for m in range(M4):
                for k in range(0, KT, 2):
                    pair = [
                        jnp.where(own_block, jnp.broadcast_to(rows[r : r + 1, :], (BT, X * ROWS)), 0.0)
                        for r in (k * M4 + m, (k + 1) * M4 + m)
                    ]
                    at = (half * M8 + up * M4 + m) * SL + k * BT
                    bd[t, at : at + 2 * BT, :] = jnp.concatenate(pair, axis=0).astype(BF16)

    def product(half, t):
        terms = jnp.dot(
            bd[t, half * M8 * SL : (half + 1) * M8 * SL, :], wk[t].reshape(X * ROWS, Q), preferred_element_type=F32
        )
        top = terms.astype(BF16)
        rest = (terms - top.astype(F32)).astype(BF16)
        where = pl.ds(pl.multiple_of(t * SL, SL), SL)
        both = jnp.concatenate([top, rest], axis=1)
        terms_of[half * M8 : (half + 1) * M8, where, :] = both.reshape(M8, SL, 2 * Q)

    def lay_out_pair(half):
        def one(i, carry):
            zz = distance(i)
            arrived(jx.at[half, pl.ds(0, X - 1), pl.ds(zz * H, H)], r_jx.at[half, zz])
            for core in range(H):
                lay_out(half, zz * H + core)
            return carry

        return one

    def products(half):
        def one(i, carry):
            zz = distance(i)
            if half == 0:
                arrived(wk.at[0], r_sb.at[zz])
            for core in range(H):
                product(half, zz * H + core)
            return carry

        return one

    close = 5
    lax.fori_loop(0, close, lay_out_pair(0), 0)
    lax.fori_loop(0, close, products(0), 0)
    for i, d in enumerate((Z - 3, 3)):
        arrived(chunk(d), r_far.at[i])
        share(d)
    arrived(wk.at[0, pl.ds(0, X // 2)], r_half.at[0])
    arrived(wk.at[0, pl.ds(0, X // 2)], r_half.at[1])
    share(Z // 2)
    lax.fori_loop(close, Z, lay_out_pair(0), 0)

    pl.semaphore_wait(ready, Y - 1)

    arrived(px.at[pl.ds(0, X - 1)], r_px)
    notes = []
    for g in range(ZH // 4):
        total = jnp.zeros((1, 128), F32)
        for i in range(X):
            for t in range(4):
                total = total + px[i, g * 4 + t]
        notes.append(total)
    slot_place = jnp.concatenate(notes, axis=1)
    line = lax.broadcasted_iota(jnp.int32, (NT, ZH * SL), 0)
    wanted = ((line % (YL * X)) * PER + line // (YL * X)).astype(F32) + 1.0
    chosen = jnp.where(wanted == slot_place, 1.0, 0.0).astype(BF16)

    for half in range(YH):
        if half == 0:
            for i in range(close, Z):
                product(0, distance(i) * H + h)
            for i in range(close, Z):
                arrived(wk.at[0], r_sb.at[distance(i)])
                product(0, distance(i) * H + (1 - h))
        else:
            lax.fori_loop(0, Z, lay_out_pair(1), 0)
            lax.fori_loop(0, Z, products(1), 0)
        for up in range(YH):
            for m in range(M4):
                here = half * M8 + up * M4 + m
                gram = jnp.dot(chosen, terms_of[here], preferred_element_type=F32)
                gy[up, m * NT : (m + 1) * NT, :] = gram[:, :Q] + gram[:, Q:]
            for c in range(YL * X):
                ysend[half, up * YL * X + c] = gy[up, pl.ds(c, M4 * PER, stride=YL * X), :].astype(BF16)

        def deliver(n, carry):
            there, across = (y + n // X) % Y, (x + n) % X
            send(
                ysend.at[half, there * X + across], yrecv.at[half, y * X + x],
                s_y.at[half], r_y.at[half], at_yx(there, across),
            )
            return carry

        for turn in (4, 3, 5, 2, 6, 1, 7):
            lax.fori_loop(turn * X, turn * X + X, deliver, 0)
        lax.fori_loop(1, X, deliver, 0)
        yrecv[half, y * X + x] = ysend[half, y * X + x]

    for half in range(2):
        arrived(yrecv.at[half, pl.ds(0, Y * X - 1)], r_y.at[half])
        for i in range(X):
            total = yrecv[half, i].astype(F32)
            for other in range(1, Y):
                total = total + yrecv[half, other * X + i].astype(F32)
            done[i, half * M4 * PER : (half + 1) * M4 * PER, :] = total
    quarters = []
    for i in range(X):
        quarters.append(jnp.concatenate([done[i, pl.ds(j, M8, stride=PER), :] for j in range(PER)], axis=0))
    gram = jnp.concatenate(quarters, axis=1)
    ghi = gram.astype(BF16)
    glo = (gram - ghi.astype(F32)).astype(BF16)

    wide = jnp.dot(jnp.concatenate([ghi, glo], axis=0), fhi[...], preferred_element_type=F32)
    low = jnp.dot(ghi, flo[...], preferred_element_type=F32)
    out[...] = (wide[: PER * M8] + (wide[PER * M8 :] + low)).reshape(PER, M8, PANEL)

    arrived(wk.at[pl.ds(0, 4)], s_w)
    arrived(wk.at[0, pl.ds(0, X - 1)], s_w0)
    for half in range(YH):
        arrived(jm.at[half, pl.ds(0, ZH - 1)], s_jz.at[half])
        arrived(jx.at[half, pl.ds(0, X - 1)], s_jx.at[half])
    arrived(px.at[x, pl.ds(0, ZH - 1)], s_pz)
    arrived(px.at[pl.ds(0, X - 1)], s_px)
    arrived(wk.at[pl.ds(0, 3)], s_h)
    arrived(wk.at[pl.ds(0, Z)], s_sb)
    for half in range(2):
        arrived(yrecv.at[half, pl.ds(0, Y * X - 1)], s_y.at[half])


def local(jac, panel_jac, weights, tile_lists, tile_masks, tile_order, factor_inverse):
    dma = pltpu.SemaphoreType.DMA
    given = (jac, panel_jac, weights[None, :], tile_lists, tile_masks, tile_order[None, :], factor_inverse)
    held = [pltpu.with_memory_space_constraint(value, pltpu.HBM) for value in given]
    return pl.pallas_call(
        kernel,
        out_shape=jax.ShapeDtypeStruct((PER, M8, PANEL), F32),
        in_specs=[pl.BlockSpec(memory_space=pltpu.HBM)] * 7,
        out_specs=pl.BlockSpec(memory_space=pltpu.VMEM),
        scratch_shapes=[
            pltpu.VMEM((ROWS, KT * TILE), BF16),
            pltpu.VMEM((ROWS, PANEL), BF16),
            pltpu.VMEM((1, ROWS), F32),
            pltpu.SMEM((NB, KT), jnp.int32),
            pltpu.SMEM((NB, KT), jnp.int32),
            pltpu.VMEM((1, NT), jnp.int32),
            pltpu.VMEM((X, ROWS, Q), BF16),
            pltpu.VMEM((ZH, X, ROWS, Q), BF16),
            pltpu.VMEM((YH, ZH, 2 * M8, 2 * ROWS), BF16),
            pltpu.VMEM((YH, X, ZH, 2 * M8, 2 * ROWS), BF16),
            pltpu.VMEM((X, ZH, 1, 128), F32),
            pltpu.VMEM((PANEL, PANEL), F32),
            pltpu.VMEM((PANEL, PANEL), BF16),
            pltpu.VMEM((PANEL, PANEL), BF16),
            pltpu.VMEM((ZH, M * SL, X * ROWS), BF16),
            pltpu.VMEM((M, ZH * SL, 2 * Q), BF16),
            pltpu.VMEM((YH, M4 * NT, Q), F32),
            pltpu.VMEM((2, Y * X, M4 * PER, Q), BF16),
            pltpu.VMEM((2, Y * X, M4 * PER, Q), BF16),
            pltpu.VMEM((X, M8 * PER, Q), F32),
            dma((7,)), dma(()), dma(()), dma((Z,)), dma((YH,)), dma((YH, Z)), dma(()), dma(()),
            dma((YH,)), dma((YH, Z)), dma(()), dma(()),
            dma(()), dma((2,)), dma((2,)), dma(()), dma((Z,)), dma((2,)), dma((2,)), pltpu.SemaphoreType.REGULAR,
        ],
        compiler_params=pltpu.CompilerParams(
            collective_id=0, has_side_effects=True, vmem_limit_bytes=48 * 1024 * 1024
        ),
    )(*held)


def solution(mesh):
    in_specs = (
        P(("rows", "cols"), None),
        P(("rows", "cols"), None),
        P(("rows", "cols")),
        P(("rows", "cols"), None),
        P(("rows", "cols"), None),
        P(),
        P(),
    )
    out_specs = P("cols", "rows", None)
    return jax.shard_map(local, mesh=mesh, in_specs=in_specs, out_specs=out_specs, check_vma=False)
```

```python
import functools

import jax
import jax.numpy as jnp
from jax import lax
from jax.experimental import pallas as pl
from jax.experimental.pallas import tpu as pltpu
from jax.sharding import PartitionSpec as P

MESH = pl.DeviceIdType.MESH
F32, BF16 = jnp.float32, jnp.bfloat16
X, YL, YH, Z, H = 4, 4, 2, 8, 2
ZH, Y = Z * H, YH * YL
KT, RB, NB, PER = 4, 32, 2, 6
ROWS, TILE, PANEL = NB * RB, 256, 512
M8 = TILE // (YH * ZH)
M = YH * M8
M4 = M8 // 2
Q = PANEL // X
BT = X * NB
SL = KT * BT
NT = X * YL * PER


def kernel(
    jac_hbm, panel_hbm, weights_hbm, lists_hbm, masks_hbm, order_hbm, finv_hbm, out,
    jac, panel, weights, lists, masks, order,
    ws, wk, jm, jx, px, finv, fhi, flo, bd, terms_of, gy, ysend, yrecv, done,
    s_in, s_w, s_w0, r_w, s_jz, r_jz, s_pz, r_pz, s_jx, r_jx, s_px, r_px,
    s_h, r_far, r_half, s_sb, r_sb, s_y, r_y, ready,
):
    inputs = [
        pltpu.make_async_copy(src, dst, s_in.at[i])
        for i, (src, dst) in enumerate([
            (panel_hbm, panel), (weights_hbm, weights), (lists_hbm, lists), (masks_hbm, masks),
            (order_hbm, order), (jac_hbm, jac), (finv_hbm, finv),
        ])
    ]
    for copy in inputs:
        copy.start()

    ri, ci = lax.axis_index("rows"), lax.axis_index("cols")
    yh, zh = ri // ZH, ri % ZH
    z, h = zh // H, zh % H
    yl, x = ci // X, ci % X
    y = yh * YL + yl

    def at_xz(dx, dz):
        return (yh * ZH + ((z + dz) % Z) * H + h, yl * X + (x + dx) % X)

    def at_x(d):
        return at_xz(d, 0)

    def at_z(d):
        return at_xz(0, d)

    def at_zh(d):
        return (yh * ZH + (zh + d) % ZH, ci)

    def at_yx(there, across):
        return ((there // YL) * ZH + zh, (there % YL) * X + across)

    sibling = (yh * ZH + z * H + (1 - h), ci)

    def send(src, dst, s, r, to):
        copy = pltpu.make_async_remote_copy(src, dst, s, r, device_id=to, device_id_type=MESH)
        copy.start()

    def arrived(ref, sem):
        pltpu.make_async_copy(ref, ref, sem).wait()

    barrier = pltpu.get_barrier_semaphore()

    def greet(n, where):
        for d in range(1, n):
            pl.semaphore_signal(barrier, inc=1, device_id=where(d), device_id_type=MESH)

    for dz in (2, Z - 2, 0, 1, Z - 1):
        greet(X, lambda d: at_xz(d, dz))
    greet(ZH, at_zh)
    greet(Y, lambda d: at_yx((y + d) % Y, x))

    inputs[0].wait()
    inputs[1].wait()
    eye = lax.broadcasted_iota(jnp.int32, (ROWS, ROWS), 0) == lax.broadcasted_iota(jnp.int32, (ROWS, ROWS), 1)
    wcol = jnp.sum(jnp.where(eye, jnp.broadcast_to(weights[...], (ROWS, ROWS)), 0.0), axis=1, keepdims=True)
    for q in range(X):
        ws[q] = (wcol * panel[:, q * Q : (q + 1) * Q].astype(F32)).astype(BF16)

    pl.semaphore_wait(barrier, 5 * (X - 1) + ZH - 1 + Y - 1)

    def near(dz, first, sem):
        def one(dx, carry):
            send(ws.at[(x + dx) % X], wk.at[zh, x], sem, r_w.at[z], at_xz(dx, dz))
            return carry

        lax.fori_loop(first, X, one, 0)

    near(2, 0, s_w)
    near(Z - 2, 0, s_w)
    near(0, 1, s_w0)
    wk[zh, x] = ws[x]

    inputs[5].wait()
    turned = []
    for k in range(KT):
        both = [jac[:, k * TILE + i * 128 : k * TILE + i * 128 + 128].astype(F32) for i in range(YH)]
        turned.append(jnp.concatenate(both, axis=0).T)
    first_four = lax.broadcasted_iota(jnp.int32, (ZH * M8, 128), 0) % M8 < M4
    for half in range(2):
        tiles = []
        for k in range(0, KT, 2):
            if half == 0:
                tile = jnp.where(first_four, turned[k], pltpu.roll(turned[k + 1], M4, 0))
            else:
                tile = jnp.where(first_four, pltpu.roll(turned[k], ZH * M8 - M4, 0), turned[k + 1])
            tiles.append(tile.reshape(ZH, M8, 128))
        jm[half] = jnp.concatenate(tiles, axis=1).astype(BF16)

    def spread(half):
        def one(d, carry):
            send(jm.at[half, (zh + d) % ZH], jx.at[half, x, zh], s_jz.at[half], r_jz.at[half, z], at_zh(d))
            return carry

        lax.fori_loop(1, ZH, one, 0)

    spread(0)

    for copy in inputs[2:5]:
        copy.wait()
    lane = lax.broadcasted_iota(jnp.int32, (1, 128), 1)
    ids = order[...]
    place = lax.broadcasted_iota(jnp.int32, (1, NT), 1).astype(F32) + 1.0
    base = (zh % 4) * SL + x * NB
    note = jnp.zeros((1, 128), F32)
    for b in range(NB):
        for k in range(KT):
            hit = jnp.sum(jnp.where(ids == lists[b, k], place, 0.0), axis=1, keepdims=True)
            hit = hit * masks[b, k].astype(F32)
            note = note + jnp.where(lane == base + k * BT + b, hit, 0.0)
    px[x, zh] = note

    def tell(d, carry):
        send(px.at[x, zh], px.at[x, zh], s_pz, r_pz, at_zh(d))
        return carry

    lax.fori_loop(1, ZH, tell, 0)
    for d in range(1, Y):
        pl.semaphore_signal(ready, inc=1, device_id=at_yx((y + d) % Y, x), device_id_type=MESH)

    spread(1)
    near(1, 0, s_w)
    near(Z - 1, 0, s_w)
    for half in range(YH):
        jx[half, x, zh] = jm[half, zh]

    inputs[6].wait()
    full = finv[...].T
    high = full.astype(BF16)
    fhi[...] = high
    flo[...] = (full - high.astype(F32)).astype(BF16)

    def chunk(d):
        return wk.at[((z + d) % Z) * H + h]

    def share(d):
        send(chunk(d), chunk(d), s_sb, r_sb.at[(z + d) % Z], sibling)


    for i, (d, first, step) in enumerate(((Z - 2, 0, 1), (2, X // 2, Z - 1))):
        arrived(chunk(d), r_w.at[(z + d) % Z])
        send(chunk(d), chunk(d), s_h, r_far.at[i], at_z(step))
        part = wk.at[((z + d) % Z) * H + h, pl.ds(first, X // 2)]
        send(part, part, s_h, r_half.at[i], at_z(2 * step))
        share(d)

    def distance(i):
        return (z + (i % 2) * ((i + 1) // 2) + (1 - i % 2) * (Z - i // 2)) % Z

    def pass_jac(half):
        def one(i, carry):
            zz = distance(i)
            mine = jx.at[half, x, pl.ds(zz * H, H)]

            @pl.when(i == 0)
            def _():
                arrived(jx.at[half, x, pl.ds(0, 1)], r_jz.at[half, zz])

            @pl.when(i > 0)
            def _():
                arrived(mine, r_jz.at[half, zz])

            for d in range(1, X):
                send(mine, mine, s_jx.at[half], r_jx.at[half, zz], at_x(d))
            return carry

        lax.fori_loop(0, Z, one, 0)

    pass_jac(0)
    arrived(px.at[x, pl.ds(0, ZH - 1)], r_pz)
    for d in range(1, X):
        send(px.at[x], px.at[x], s_px, r_px, at_x(d))
    arrived(wk.at[0, pl.ds(0, X - 1)], r_w.at[z])
    share(0)
    for d in (Z - 1, 1):
        arrived(chunk(d), r_w.at[(z + d) % Z])
        share(d)
    pass_jac(1)

    low_lanes = lax.broadcasted_iota(jnp.int32, (2 * M8, 128), 1) < ROWS
    own_block = (lax.broadcasted_iota(jnp.int32, (BT, X * ROWS), 1) // RB) == lax.broadcasted_iota(
        jnp.int32, (BT, X * ROWS), 0
    )

    def lay_out(half, t):
        parts = [jx[half, i, t].astype(F32) for i in range(X)]
        swapped = [pltpu.roll(v, ROWS, 1) for v in parts]
        for up in range(YH):
            if up == 0:
                tiles = [jnp.where(low_lanes, parts[i], swapped[i + 1]) for i in range(0, X, 2)]
            else:
                tiles = [jnp.where(low_lanes, swapped[i], parts[i + 1]) for i in range(0, X, 2)]
            rows = jnp.concatenate(tiles, axis=1)
            for m in range(M4):
                for k in range(0, KT, 2):
                    pair = [
                        jnp.where(own_block, jnp.broadcast_to(rows[r : r + 1, :], (BT, X * ROWS)), 0.0)
                        for r in (k * M4 + m, (k + 1) * M4 + m)
                    ]
                    at = (half * M8 + up * M4 + m) * SL + k * BT
                    bd[t, at : at + 2 * BT, :] = jnp.concatenate(pair, axis=0).astype(BF16)

    def product(half, t):
        terms = jnp.dot(
            bd[t, half * M8 * SL : (half + 1) * M8 * SL, :], wk[t].reshape(X * ROWS, Q), preferred_element_type=F32
        )
        top = terms.astype(BF16)
        rest = (terms - top.astype(F32)).astype(BF16)
        where = pl.ds(pl.multiple_of(t * SL, SL), SL)
        both = jnp.concatenate([top, rest], axis=1)
        terms_of[half * M8 : (half + 1) * M8, where, :] = both.reshape(M8, SL, 2 * Q)

    def lay_out_pair(half):
        def one(i, carry):
            zz = distance(i)
            arrived(jx.at[half, pl.ds(0, X - 1), pl.ds(zz * H, H)], r_jx.at[half, zz])
            for core in range(H):
                lay_out(half, zz * H + core)
            return carry

        return one

    def products(half):
        def one(i, carry):
            zz = distance(i)
            if half == 0:
                arrived(wk.at[0], r_sb.at[zz])
            for core in range(H):
                product(half, zz * H + core)
            return carry

        return one

    close = 5
    lax.fori_loop(0, close, lay_out_pair(0), 0)
    lax.fori_loop(0, close, products(0), 0)
    for i, d in enumerate((Z - 3, 3)):
        arrived(chunk(d), r_far.at[i])
        share(d)
    arrived(wk.at[0, pl.ds(0, X // 2)], r_half.at[0])
    arrived(wk.at[0, pl.ds(0, X // 2)], r_half.at[1])
    share(Z // 2)
    lax.fori_loop(close, Z, lay_out_pair(0), 0)

    pl.semaphore_wait(ready, Y - 1)

    arrived(px.at[pl.ds(0, X - 1)], r_px)
    notes = []
    for g in range(ZH // 4):
        total = jnp.zeros((1, 128), F32)
        for i in range(X):
            for t in range(4):
                total = total + px[i, g * 4 + t]
        notes.append(total)
    slot_place = jnp.concatenate(notes, axis=1)
    line = lax.broadcasted_iota(jnp.int32, (NT, ZH * SL), 0)
    wanted = ((line % (YL * X)) * PER + line // (YL * X)).astype(F32) + 1.0
    chosen = jnp.where(wanted == slot_place, 1.0, 0.0).astype(BF16)

    for half in range(YH):
        if half == 0:
            for i in range(close, Z):
                product(0, distance(i) * H + h)
            for i in range(close, Z):
                arrived(wk.at[0], r_sb.at[distance(i)])
                product(0, distance(i) * H + (1 - h))
        else:
            lax.fori_loop(0, Z, lay_out_pair(1), 0)
            for i in range(Z):
                products(1)(i, 0)
        for up in range(YH):
            for m in range(M4):
                here = half * M8 + up * M4 + m
                gram = jnp.dot(chosen, terms_of[here], preferred_element_type=F32)
                gy[up, m * NT : (m + 1) * NT, :] = gram[:, :Q] + gram[:, Q:]
            for c in range(YL * X):
                ysend[half, up * YL * X + c] = gy[up, pl.ds(c, M4 * PER, stride=YL * X), :].astype(BF16)

        def deliver(n, carry):
            there, across = (y + n // X) % Y, (x + n) % X
            send(
                ysend.at[half, there * X + across], yrecv.at[half, y * X + x],
                s_y.at[half], r_y.at[half], at_yx(there, across),
            )
            return carry

        for turn in (4, 3, 5, 2, 6, 1, 7):
            lax.fori_loop(turn * X, turn * X + X, deliver, 0)
        lax.fori_loop(1, X, deliver, 0)
        yrecv[half, y * X + x] = ysend[half, y * X + x]

    for half in range(2):
        arrived(yrecv.at[half, pl.ds(0, Y * X - 1)], r_y.at[half])
        for i in range(X):
            total = yrecv[half, i].astype(F32)
            for other in range(1, Y):
                total = total + yrecv[half, other * X + i].astype(F32)
            done[i, half * M4 * PER : (half + 1) * M4 * PER, :] = total
    quarters = []
    for i in range(X):
        quarters.append(jnp.concatenate([done[i, pl.ds(j, M8, stride=PER), :] for j in range(PER)], axis=0))
    gram = jnp.concatenate(quarters, axis=1)
    ghi = gram.astype(BF16)
    glo = (gram - ghi.astype(F32)).astype(BF16)

    wide = jnp.dot(jnp.concatenate([ghi, glo], axis=0), fhi[...], preferred_element_type=F32)
    low = jnp.dot(ghi, flo[...], preferred_element_type=F32)
    out[...] = (wide[: PER * M8] + (wide[PER * M8 :] + low)).reshape(PER, M8, PANEL)

    arrived(wk.at[pl.ds(0, 4)], s_w)
    arrived(wk.at[0, pl.ds(0, X - 1)], s_w0)
    for half in range(YH):
        arrived(jm.at[half, pl.ds(0, ZH - 1)], s_jz.at[half])
        arrived(jx.at[half, pl.ds(0, X - 1)], s_jx.at[half])
    arrived(px.at[x, pl.ds(0, ZH - 1)], s_pz)
    arrived(px.at[pl.ds(0, X - 1)], s_px)
    arrived(wk.at[pl.ds(0, 3)], s_h)
    arrived(wk.at[pl.ds(0, Z)], s_sb)
    for half in range(2):
        arrived(yrecv.at[half, pl.ds(0, Y * X - 1)], s_y.at[half])


def local(jac, panel_jac, weights, tile_lists, tile_masks, tile_order, factor_inverse):
    dma = pltpu.SemaphoreType.DMA
    given = (jac, panel_jac, weights[None, :], tile_lists, tile_masks, tile_order[None, :], factor_inverse)
    held = [pltpu.with_memory_space_constraint(value, pltpu.HBM) for value in given]
    return pl.pallas_call(
        kernel,
        out_shape=jax.ShapeDtypeStruct((PER, M8, PANEL), F32),
        in_specs=[pl.BlockSpec(memory_space=pltpu.HBM)] * 7,
        out_specs=pl.BlockSpec(memory_space=pltpu.VMEM),
        scratch_shapes=[
            pltpu.VMEM((ROWS, KT * TILE), BF16),
            pltpu.VMEM((ROWS, PANEL), BF16),
            pltpu.VMEM((1, ROWS), F32),
            pltpu.SMEM((NB, KT), jnp.int32),
            pltpu.SMEM((NB, KT), jnp.int32),
            pltpu.VMEM((1, NT), jnp.int32),
            pltpu.VMEM((X, ROWS, Q), BF16),
            pltpu.VMEM((ZH, X, ROWS, Q), BF16),
            pltpu.VMEM((YH, ZH, 2 * M8, 2 * ROWS), BF16),
            pltpu.VMEM((YH, X, ZH, 2 * M8, 2 * ROWS), BF16),
            pltpu.VMEM((X, ZH, 1, 128), F32),
            pltpu.VMEM((PANEL, PANEL), F32),
            pltpu.VMEM((PANEL, PANEL), BF16),
            pltpu.VMEM((PANEL, PANEL), BF16),
            pltpu.VMEM((ZH, M * SL, X * ROWS), BF16),
            pltpu.VMEM((M, ZH * SL, 2 * Q), BF16),
            pltpu.VMEM((YH, M4 * NT, Q), F32),
            pltpu.VMEM((2, Y * X, M4 * PER, Q), BF16),
            pltpu.VMEM((2, Y * X, M4 * PER, Q), BF16),
            pltpu.VMEM((X, M8 * PER, Q), F32),
            dma((7,)), dma(()), dma(()), dma((Z,)), dma((YH,)), dma((YH, Z)), dma(()), dma(()),
            dma((YH,)), dma((YH, Z)), dma(()), dma(()),
            dma(()), dma((2,)), dma((2,)), dma(()), dma((Z,)), dma((2,)), dma((2,)), pltpu.SemaphoreType.REGULAR,
        ],
        compiler_params=pltpu.CompilerParams(
            collective_id=0, has_side_effects=True, vmem_limit_bytes=48 * 1024 * 1024
        ),
    )(*held)


def solution(mesh):
    in_specs = (
        P(("rows", "cols"), None),
        P(("rows", "cols"), None),
        P(("rows", "cols")),
        P(("rows", "cols"), None),
        P(("rows", "cols"), None),
        P(),
        P(),
    )
    out_specs = P("cols", "rows", None)
    return jax.shard_map(local, mesh=mesh, in_specs=in_specs, out_specs=out_specs, check_vma=False)
```
